32 devices in a mesh: segment: 4 (over y, x), space: 8 (over z, core).
Axes of the slice: x: 2, y: 2, z: 4, core: 2. Of those that a mesh axis runs over, the one named last changes fastest.
Arguments:
- features: bfloat16 [96, 2048], P(None, 'space'), may hold values from -6 to 6
- weights: bfloat16 [4, 27, 96, 96], P('segment'), may hold values from -0.125 to 0.125
- row_map: int32 [27, 2048], P(None, 'space'), may hold values from 0 to 512, as said below
- block_count: int32 [8], P('space'), may hold values from 2 to 2, as said below
- cotangent: bfloat16 [96, 2048], P(None, 'space'), may hold values from -6 to 6
Outputs:
- acts: bfloat16 [4, 96, 2048], P('segment', None, 'space')
- grad_in: bfloat16 [4, 96, 2048], P('segment', None, 'space')
- wgrad: float32 [4, 27, 96, 96], P('segment')
The draws below stay inside these ranges and needn't reach their ends.
Inputs may be any that keep to these rules, and one draw needn't show every extreme that they name: block_count[p] counts the live blocks of owner p; blocks at and after it are padding. Some owner has 2 live blocks. `row_map`: the value 2 * 128 + 256 means that no input feeds the row; every padding row has it for all offsets. No entry names a padding row of the owner, and no entry names a face of a neighbour that does not exist.
All inputs are finite; a program needn't handle non-finite values.
Results may differ from the reference program's by a relative error of at most 0.015.
Values may be sent and summed in bfloat16 or wider, within the bound.
No kernel may reach another device: no remote copies, remote signals or barrier semaphores. Data moves between devices by JAX's collectives and lax.ppermute only.
A program may use at most 64 MiB of HBM per device.

```python
import jax
import jax.numpy as jnp
from jax import lax

C = 96
K = 27
BLK = 2
SEGMENTS = 4
ROWS = 2048
N_SEGMENT = 4
N_SPACE = 8


def occupancy(key):
    base = jax.random.fold_in(key, 7)
    key_one, key_two = jax.random.split(base, 2)
    counts = jnp.min(jax.random.randint(key_one, (3, N_SPACE), 2, BLK + 1), axis=0)
    busiest = jax.random.randint(key_two, (), 0, N_SPACE)
    counts = jnp.where(jnp.arange(N_SPACE) == busiest, BLK, counts)
    return counts.astype(jnp.int32)


def draw_block_count(key, part):
    return occupancy(key)


def draw_row_map(key, part):
    counts = occupancy(key)
    shard_rows = BLK * 128
    all_rows = shard_rows * N_SPACE
    base = jax.random.fold_in(key, 11)
    key_one, key_two, key_three = jax.random.split(base, 3)
    column = jnp.arange(all_rows, dtype=jnp.int32)[None, :]
    owners = column // shard_rows
    position = column % shard_rows
    offsets = jnp.arange(K, dtype=jnp.int32)[:, None]
    owner_live = counts[owners] * 128
    live_mask = position < owner_live
    present = jax.random.randint(key_one, (K, all_rows), 0, 10) < 3
    center = offsets == K // 2
    local_pick = 128 + jax.random.randint(key_two, (K, all_rows), 0, 1 << 20) % owner_live
    face_pick = jax.random.randint(key_three, (K, all_rows), 0, 128)
    low_face = (position < 128) & (offsets < K // 3) & (owners > 0)
    high_face = (position >= 128) & (position < 256) & (offsets >= K - K // 3) & (owners < N_SPACE - 1)
    chosen = jnp.where(center, 128 + position, jnp.where(low_face, face_pick, jnp.where(high_face, 128 + shard_rows + face_pick, local_pick)))
    chosen = jnp.where((present | center) & live_mask, chosen, shard_rows + 256)
    return chosen.astype(jnp.int32)


def levels(stream_key, dims, shards, smallest, largest):
    level = 1.0
    for dim, parts in shards:
        heights = jax.random.uniform(jax.random.fold_in(jax.random.fold_in(stream_key, 6), dim), (parts,), jnp.float32, smallest / len(shards), largest / len(shards))
        level = level * jnp.repeat(jnp.exp(heights), dims[dim] // parts).reshape((-1,) + (1,) * (len(dims) - 1 - dim))
    return level


def gaussian(stream_key, shape, spread, reach, shards=(), kind=jnp.bfloat16):
    drawn = jax.random.normal(stream_key, shape, jnp.float32) * spread
    if len(shards) > 0:
        drawn = levels(stream_key, shape, shards, -0.22, 0.18) * drawn
    return jnp.clip(drawn, min=-reach, max=reach).astype(kind)


def setup_inputs(seed: int = 0) -> dict:
    key_list = jax.random.split(jax.random.key(seed), 6)
    return {
        "features": gaussian(key_list[0], (C, ROWS), 1.0, 6.0, ((1, 8),)),
        "weights": gaussian(key_list[1], (SEGMENTS, K, C, C), (K * C) ** -0.5, 0.125, ((0, 4),)),
        "row_map": draw_row_map(jax.random.fold_in(key_list[5], 71), 0),
        "block_count": draw_block_count(jax.random.fold_in(key_list[5], 71), 0),
        "cotangent": gaussian(key_list[4], (C, ROWS), 1.0, 6.0, ((1, 8),)),
    }


def rms_scale(inputs32):
    return lax.rsqrt(lax.optimization_barrier(jnp.mean(inputs32 * inputs32, axis=0, keepdims=True)) + 1e-05)

def silu_slope(preact):
    sigmoid_val = jax.nn.sigmoid(preact)
    return sigmoid_val * (1.0 + preact * (1.0 - sigmoid_val))

def reference(features, weights, row_map, block_count, cotangent):
    shard_rows = BLK * 128
    all_rows = shard_rows * N_SPACE
    channels = features.shape[0]
    column = jnp.arange(all_rows, dtype=jnp.int32)
    owners = column // shard_rows
    local_index = row_map
    prev_col = (owners - 1) * shard_rows + 128 + local_index
    mine_col = owners * shard_rows + local_index - 128
    next_col = (owners + 1) * shard_rows + local_index - 128 - shard_rows
    global_index = jnp.where(local_index < 128, jnp.where(owners > 0, prev_col, all_rows), jnp.where(local_index < 128 + shard_rows, mine_col, jnp.where((local_index < shard_rows + 256) & (owners < N_SPACE - 1), next_col, all_rows)))
    global_index = global_index.astype(jnp.int32)
    live_mask = (column % shard_rows < block_count[owners] * 128)[None, :]
    current = jnp.where(live_mask, features, jnp.zeros_like(features))
    saved = []
    outputs = []
    for layer in range(N_SEGMENT):
        inputs32 = current.astype(jnp.float32)
        normed = (inputs32 * rms_scale(inputs32)).astype(jnp.bfloat16)
        extended = jnp.concatenate([normed, jnp.zeros((channels, 1), jnp.bfloat16)], axis=1)
        extended32 = extended.astype(jnp.float32)
        layer_weights = weights[layer].astype(jnp.float32)

        def add_term(accum, operands):
            weight_slice, indices = operands
            return (accum + jnp.dot(weight_slice.T, extended32[:, indices], preferred_element_type=jnp.float32), None)
        preact, _ = lax.scan(add_term, jnp.zeros((channels, all_rows), jnp.float32), (layer_weights, global_index))
        preact = jnp.where(live_mask, preact, jnp.float32(0.0))
        result = (inputs32 + jax.nn.silu(preact)).astype(jnp.bfloat16)
        saved.append((current, extended32, preact))
        outputs.append(result)
        current = result
    gradient = jnp.where(live_mask, cotangent.astype(jnp.float32), jnp.float32(0.0))
    grads_in = [None] * N_SEGMENT
    weight_grads = [None] * N_SEGMENT
    for layer in reversed(range(N_SEGMENT)):
        segment_input, extended32, preact = saved[layer]
        slopes = (gradient * silu_slope(preact)).astype(jnp.bfloat16).astype(jnp.float32)
        layer_weights = weights[layer].astype(jnp.float32)

        def back_term(accum, operands):
            weight_slice, indices = operands
            accum = accum.at[:, indices].add(jnp.dot(weight_slice, slopes, preferred_element_type=jnp.float32))
            return (accum, jnp.dot(extended32[:, indices], slopes.T, preferred_element_type=jnp.float32))
        table_grad, weight_grad = lax.scan(back_term, jnp.zeros((channels, all_rows + 1), jnp.float32), (layer_weights, global_index))
        dnormed = table_grad[:, :all_rows]
        inputs32 = segment_input.astype(jnp.float32)
        inverse_rms = rms_scale(inputs32)
        dinput = inverse_rms * dnormed - inputs32 * (inverse_rms * inverse_rms * inverse_rms) * lax.optimization_barrier(jnp.mean(inputs32 * dnormed, axis=0, keepdims=True))
        gradient = gradient + dinput
        grads_in[layer] = gradient.astype(jnp.bfloat16)
        weight_grads[layer] = weight_grad * (1.0 / jnp.sqrt(jnp.float32(all_rows)))
    return (jnp.stack(outputs), jnp.stack(grads_in), jnp.stack(weight_grads))
```

```python
import functools
import math

import jax
import jax.numpy as jnp
from jax import lax
from jax.experimental import pallas as pl
from jax.experimental.pallas import tpu as pltpu
from jax.sharding import PartitionSpec as P

AXES = ("segment", "space")
BF16 = jnp.bfloat16
F32 = jnp.float32
LANES = 128
VMEM = pl.BlockSpec(memory_space=pltpu.VMEM)


def call(body, name, out_shape, *args, limit=8 << 20, scratch=(), flops=0):
    return pl.pallas_call(
        body,
        name=name,
        out_shape=out_shape,
        in_specs=[VMEM] * len(args),
        out_specs=jax.tree.map(lambda _: VMEM, out_shape),
        scratch_shapes=list(scratch),
        compiler_params=pltpu.CompilerParams(vmem_limit_bytes=limit),
        cost_estimate=pl.CostEstimate(flops=flops, bytes_accessed=0, transcendentals=0),
    )(*args)


def struct(shape, dtype):
    return jax.ShapeDtypeStruct(shape, dtype)


def swap(pairs):
    return sorted(pairs + [(target, source) for source, target in pairs])


def hop_pairs(source, target, segments, count):
    idle = [s for s in range(segments) if s not in (source, target)]
    if source > target:
        idle = idle[::-1]

    def at(segment, owner):
        return segment * count + owner

    own, down, up = [], [], []
    groups = [(source, target)] + [tuple(idle[i : i + 2]) for i in range(0, len(idle), 2)]
    for a, b in groups:
        own += [(at(a, p), at(b, p)) for p in range(count)]
        down += [(at(a, p), at(b, p - 1)) for p in range(1, count)]
        up += [(at(a, p), at(b, p + 1)) for p in range(count - 1)]
    (a, b), (c, d) = groups
    last = count - 1
    down += [(at(a, 0), at(c, 0)), (at(b, last), at(d, last))]
    up += [(at(a, last), at(c, last)), (at(b, 0), at(d, 0))]
    return swap(own), swap(down), swap(up)


def halo_pairs(segments, count):
    last = count - 1
    one, two = [], []
    for even in range(0, segments, 2):
        a, b = even * count, (even + 1) * count
        one += [(a + p, a + p + 1) for p in range(last)] + [(a + last, b + last)]
        one += [(b + p, b + p - 1) for p in range(1, count)] + [(b, a)]
        two += [(a + p, a + p - 1) for p in range(1, count)] + [(a, b)]
        two += [(b + p, b + p + 1) for p in range(last)] + [(b + last, a + last)]
    return sorted(one), sorted(two)


def rms_scale(x32):
    return lax.rsqrt(jnp.mean(x32 * x32, axis=0, keepdims=True) + 1e-5)


def normalized(x):
    x32 = x.astype(F32)
    return (x32 * rms_scale(x32)).astype(BF16)


def stacked_lookup(low, own, high):
    first = jnp.concatenate([low, own[:, :LANES]], axis=1)
    second = jnp.concatenate([own[:, LANES:], high], axis=1)
    return jnp.concatenate([first, second], axis=0)


def one_hot(columns, missing):
    half = columns.shape[1]
    within = jnp.where(columns >= missing, -1, jnp.bitwise_and(columns, half - 1))
    places = lax.broadcasted_iota(jnp.int32, (half, half), 0).astype(F32).astype(BF16)
    within = within.astype(F32).astype(BF16)
    return jnp.where(places == within, jnp.ones((), BF16), jnp.zeros((), BF16))


def pick_rows(lookup, columns):
    channels, half = lookup.shape[0] // 2, lookup.shape[1]
    found = jnp.dot(lookup, one_hot(columns, 2 * half), preferred_element_type=F32)
    return jnp.where(columns >= half, found[channels:], found[:channels]).astype(BF16)


def silu_slope(z):
    sigmoid = jax.nn.sigmoid(z)
    return sigmoid * (1.0 + z * (1.0 - sigmoid))


def through_norm(x32, grad):
    inverse = rms_scale(x32)
    mean = jnp.mean(x32 * grad, axis=0, keepdims=True)
    return inverse * grad - x32 * (inverse * inverse * inverse) * mean


def prepare_kernel(features, cotangent, live, x, one, two, grad):
    even = lax.rem(lax.axis_index("segment"), 2) == 0
    keep = live[...] > 0.0
    zero = jnp.zeros((), F32)
    rows = jnp.where(keep, features[...].astype(F32), zero).astype(BF16)
    x[...] = rows
    low, high = rows[:, :LANES], rows[:, LANES:]
    up = jnp.where(even, 1.0, 0.0).astype(F32) > 0.5
    one[...] = jnp.where(up, high, low)
    two[...] = jnp.where(up, low, high)
    grad[...] = jnp.where(keep, cotangent[...].astype(F32), zero)


def forward_body(own, low, high, weight, row_map, live, z, out, out_low, out_high, picked):
    offsets, channels = weight.shape[0], weight.shape[1]
    lookup = stacked_lookup(normalized(low), normalized(own), normalized(high))
    for k in range(offsets):
        picked[k * channels : (k + 1) * channels, :] = pick_rows(lookup, row_map[k : k + 1, :])
    total = lax.dot_general(
        weight[...].reshape(offsets * channels, channels),
        picked[...],
        (((0,), (0,)), ((), ())),
        preferred_element_type=F32,
    )
    total = jnp.where(live[...] > 0.0, total, jnp.zeros((), F32))
    z[...] = total
    result = (own.astype(F32) + total * jax.nn.sigmoid(total)).astype(BF16)
    out[...] = result
    out_low[...] = result[:, :LANES]
    out_high[...] = result[:, LANES:]


def forward_kernel(turn, *refs):
    (own, low, high, weight, row_map, live, z_in, x_in, act_in) = refs[:9]
    (out, out_low, out_high, z, x, act, picked) = refs[9:]
    active = lax.axis_index("segment") == turn

    @pl.when(active)
    def _():
        forward_body(
            own[...], low[...], high[...], weight, row_map, live, z, out, out_low, out_high, picked
        )
        x[...] = own[...]
        act[...] = out[...]

    @pl.when(jnp.logical_not(active))
    def _():
        out[...] = own[...]
        out_low[...] = low[...]
        out_high[...] = high[...]
        z[...] = z_in[...]
        x[...] = x_in[...]
        act[...] = act_in[...]


def spread_body(dz, weight, row_map, masked, hot):
    offsets, channels = weight.shape[0], weight.shape[1]
    half = row_map.shape[1]
    for k in range(offsets):
        columns = row_map[k : k + 1, :]
        rows = jnp.dot(weight[k], dz, preferred_element_type=F32)
        upper = columns >= half
        zero = jnp.zeros((), F32)
        masked[:channels, k * half : (k + 1) * half] = jnp.where(upper, zero, rows).astype(BF16)
        masked[channels:, k * half : (k + 1) * half] = jnp.where(upper, rows, zero).astype(BF16)
        hot[:, k * half : (k + 1) * half] = one_hot(columns, 2 * half)
    return lax.dot_general(
        masked[...], hot[...], (((1,), (1,)), ((), ())), preferred_element_type=F32
    )


def face_terms(x, from_low, from_high):
    owner, count = lax.axis_index("space"), lax.axis_size("space")
    zero = jnp.zeros((), F32)
    lane = lax.broadcasted_iota(jnp.int32, (1, LANES), 1)
    has_low = lane + owner * LANES >= LANES
    has_high = lane + (owner + 1) * LANES < count * LANES
    low = jnp.where(has_low, from_low.astype(F32), zero)
    high = jnp.where(has_high, from_high.astype(F32), zero)
    return through_norm(x.astype(F32), jnp.concatenate([low, high], axis=1))


def slope_kernel(turn, segments, part_in, from_low, from_high, act, z, grad_in, dz_in, dz, grad):
    active = lax.axis_index("segment") == turn

    @pl.when(active)
    def _():
        if turn == segments - 1:
            total = grad_in[...]
        else:
            total = part_in[...].astype(F32) + face_terms(act[...], from_low[...], from_high[...])
        grad[...] = total
        dz[...] = (total * silu_slope(z[...])).astype(BF16)

    @pl.when(jnp.logical_not(active))
    def _():
        dz[...] = dz_in[...]
        grad[...] = grad_in[...]


def spread_kernel(turn, dz, grad, x, weight, row_map, part_in, low_in, high_in, *refs):
    (part, send, low, high, masked, hot) = refs
    active = lax.axis_index("segment") == turn

    @pl.when(active)
    def _():
        channels = x.shape[0]
        table = spread_body(dz[...], weight, row_map, masked, hot)
        own = jnp.concatenate([table[:channels, LANES:], table[channels:, :LANES]], axis=1)
        total = grad[...] + through_norm(x[...].astype(F32), own)
        part[...] = total
        send[...] = total.astype(BF16)
        low[...] = table[:channels, :LANES].astype(BF16)
        high[...] = table[channels:, LANES:].astype(BF16)

    @pl.when(jnp.logical_not(active))
    def _():
        part[...] = part_in[...]
        send[...] = part_in[...].astype(BF16)
        low[...] = low_in[...]
        high[...] = high_in[...]


def order_kernel(low, high, one, two):
    even = jnp.where(lax.rem(lax.axis_index("segment"), 2) == 0, 1.0, 0.0).astype(F32) > 0.5
    one[...] = jnp.where(even, high[...], low[...])
    two[...] = jnp.where(even, low[...], high[...])


def finish_kernel(part, x, one, two, out):
    even = jnp.where(lax.rem(lax.axis_index("segment"), 2) == 0, 1.0, 0.0).astype(F32) > 0.5
    from_low = jnp.where(even, one[...], two[...])
    from_high = jnp.where(even, two[...], one[...])
    out[...] = (part[...] + face_terms(x[...], from_low, from_high)).astype(BF16)


def picked_kernel(channels, x_all, map_all, picked):
    owners, rows = x_all.shape[0], x_all.shape[2]
    offsets = map_all.shape[1]
    me = lax.axis_index("space")
    for block in range(owners):
        q = jnp.bitwise_xor(me, block_distance(block, owners))
        low = x_all[jnp.maximum(q - 1, 0)][:, LANES:]
        high = x_all[jnp.minimum(q + 1, owners - 1)][:, :LANES]
        lookup = stacked_lookup(normalized(low), normalized(x_all[q]), normalized(high))
        columns = map_all[q]
        for k in range(offsets):
            picked[k * channels : (k + 1) * channels, block * rows : (block + 1) * rows] = (
                pick_rows(lookup, columns[k : k + 1, :])
            )


def block_distance(block, owners):
    return 2 * (block % (owners // 2)) + block // (owners // 2)


def join_kernel(*refs):
    for place, ref in enumerate(refs[:-1]):
        refs[-1][place] = ref[...]


def weight_kernel(factor, picked, *refs):
    out = refs[-1]
    slopes = [ref[i] for ref in refs[:-1] for i in range(ref.shape[0])]
    slopes = jnp.concatenate(slopes, axis=1)
    offsets, channels = out.shape[0], out.shape[1]
    for k in range(offsets):
        out[k] = factor * lax.dot_general(
            picked[k * channels : (k + 1) * channels, :],
            slopes,
            (((1,), (1,)), ((), ())),
            preferred_element_type=F32,
        )


def lone_picked_kernel(low, own, high, row_map, picked):
    channels = own.shape[0]
    lookup = stacked_lookup(normalized(low[...]), normalized(own[...]), normalized(high[...]))
    for k in range(row_map.shape[0]):
        picked[k * channels : (k + 1) * channels, :] = pick_rows(lookup, row_map[k : k + 1, :])


def per_device(features, weights, row_map, block_count, cotangent):
    channels, rows = features.shape
    segments, count = lax.axis_size("segment"), lax.axis_size("space")
    offsets = row_map.shape[0]
    weight = weights[0]
    wide, face = (channels, rows), (channels, LANES)
    live = (jnp.arange(rows, dtype=jnp.int32) < block_count[0] * LANES).astype(F32)[None, :]
    current, one, two, grad = call(
        prepare_kernel,
        "prepare",
        [struct(wide, BF16), struct(face, BF16), struct(face, BF16), struct(wide, F32)],
        features,
        cotangent,
        live,
    )
    first, second = halo_pairs(segments, count)
    low, high = lax.ppermute(one, AXES, first), lax.ppermute(two, AXES, second)

    flops = 2 * offsets * channels * channels * rows
    z = jnp.zeros(wide, F32)
    x = act = current
    own = current
    for turn in range(segments):
        own, low, high, z, x, act = call(
            functools.partial(forward_kernel, turn),
            f"forward{turn}",
            [
                struct(wide, BF16),
                struct(face, BF16),
                struct(face, BF16),
                struct(wide, F32),
                struct(wide, BF16),
                struct(wide, BF16),
            ],
            own,
            low,
            high,
            weight,
            row_map,
            live,
            z,
            x,
            act,
            scratch=[pltpu.VMEM((offsets * channels, rows), BF16)],
            flops=flops,
        )
        if turn + 1 < segments:
            straight, down, up = hop_pairs(turn, turn + 1, segments, count)
            own, from_down, from_up = (
                lax.ppermute(own, AXES, straight),
                lax.ppermute(low, AXES, down),
                lax.ppermute(high, AXES, up),
            )
            low, high = from_up, from_down

    everyone = count <= 16
    if everyone:
        x_all = lax.all_gather(x, "space", axis=0)
        map_all = lax.all_gather(row_map, "space", axis=0)

    dz = jnp.zeros(wide, BF16)
    part = grad
    send, from_low, from_high = own, low, high
    out_low, out_high = low, high
    for turn in reversed(range(segments)):
        dz, grad = call(
            functools.partial(slope_kernel, turn, segments),
            f"slope{turn}",
            [struct(wide, BF16), struct(wide, F32)],
            send,
            from_low,
            from_high,
            act,
            z,
            grad,
            dz,
        )
        if turn == 0 and everyone:
            chips = [
                lax.ppermute(dz, "space", [(p, p ^ (2 * m)) for p in range(count)])
                for m in range(1, count // 2)
            ]
        part, send, out_low, out_high = call(
            functools.partial(spread_kernel, turn),
            f"spread{turn}",
            [struct(wide, F32), struct(wide, BF16), struct(face, BF16), struct(face, BF16)],
            dz,
            grad,
            x,
            weight,
            row_map,
            part,
            out_low,
            out_high,
            scratch=[
                pltpu.VMEM((2 * channels, offsets * rows), BF16),
                pltpu.VMEM((rows, offsets * rows), BF16),
            ],
            limit=16 << 20,
            flops=2 * flops,
        )
        if turn > 0:
            straight, down, up = hop_pairs(turn, turn - 1, segments, count)
            send, from_high, from_low = (
                lax.ppermute(send, AXES, straight),
                lax.ppermute(out_low, AXES, down),
                lax.ppermute(out_high, AXES, up),
            )

    one, two = call(
        order_kernel, "order", [struct(face, BF16), struct(face, BF16)], out_low, out_high
    )
    one, two = lax.ppermute(one, AXES, first), lax.ppermute(two, AXES, second)
    grad_in = call(finish_kernel, "finish", struct(wide, BF16), part, x, one, two)

    factor = 1.0 / math.sqrt(rows * count)
    shape = struct((offsets, channels, channels), F32)
    if everyone:
        picked = call(
            functools.partial(picked_kernel, channels),
            "picked",
            struct((offsets * channels, count * rows), BF16),
            x_all,
            map_all,
            limit=24 << 20,
            flops=8 * flops,
        )
        mine = call(join_kernel, "join", struct((count // 2,) + wide, BF16), dz, *chips)
        other = lax.ppermute(mine, "space", [(p, p ^ 1) for p in range(count)])
        weight_grad = call(
            functools.partial(weight_kernel, factor),
            "weight_grad",
            shape,
            picked,
            mine,
            other,
            limit=24 << 20,
            flops=8 * flops,
        )
    else:
        low = lax.ppermute(x[:, LANES:], "space", [(p, p + 1) for p in range(count - 1)])
        high = lax.ppermute(x[:, :LANES], "space", [(p, p - 1) for p in range(1, count)])
        picked = call(
            lone_picked_kernel,
            "lone_picked",
            struct((offsets * channels, rows), BF16),
            low,
            x,
            high,
            row_map,
        )
        weight_grad = call(
            functools.partial(weight_kernel, factor), "weight_grad", shape, picked, dz[None]
        )
        weight_grad = lax.psum(weight_grad, "space")
    return act[None], grad_in[None], weight_grad[None]


def solution(mesh):
    placed = (
        P(None, "space"),
        P("segment", None, None, None),
        P(None, "space"),
        P("space"),
        P(None, "space"),
    )
    return jax.shard_map(
        per_device,
        mesh=mesh,
        in_specs=placed,
        out_specs=(
            P("segment", None, "space"),
            P("segment", None, "space"),
            P("segment", None, None, None),
        ),
        check_vma=False,
    )
```

```python
import functools
import math

import jax
import jax.numpy as jnp
from jax import lax
from jax.experimental import pallas as pl
from jax.experimental.pallas import tpu as pltpu
from jax.sharding import PartitionSpec as P

AXES = ("segment", "space")
BF16 = jnp.bfloat16
F32 = jnp.float32
LANES = 128
VMEM = pl.BlockSpec(memory_space=pltpu.VMEM)
HBM = pl.BlockSpec(memory_space=pltpu.HBM)


def call(body, name, out_shape, *args, limit=8 << 20, scratch=(), flops=0, far=0, aliases=None):
    return pl.pallas_call(
        body,
        name=name,
        out_shape=out_shape,
        in_specs=[HBM] * far + [VMEM] * (len(args) - far),
        out_specs=jax.tree.map(lambda _: VMEM, out_shape),
        scratch_shapes=list(scratch),
        input_output_aliases=aliases or {},
        compiler_params=pltpu.CompilerParams(vmem_limit_bytes=limit),
        cost_estimate=pl.CostEstimate(flops=flops, bytes_accessed=0, transcendentals=0),
    )(*args)


def after(value, *others):
    return lax.optimization_barrier((value,) + others)[0]


def after_all(values, others):
    return lax.optimization_barrier((*values, *others))[: len(values)]


def struct(shape, dtype):
    return jax.ShapeDtypeStruct(shape, dtype)


BESIDE_OWN = (
    (2, ((2, 2, 1), (3, 3, 1))),
    (0, ((3, 0, 6), (0, 3, 0))),
    (0, ((0, 1, 2), (1, 0, 0))),
    (2, ((1, 1, 6), (0, 0, 1))),
    (2, ((3, 3, 6), (0, 0, 1))),
    (0, ((2, 2, 6), (3, 3, 1))),
)
BESIDE_FACES = (
    (4, (2, 2), ((3, 3, 1),)),
    (0, (3, 3), ((0, 0, 1),)),
    (0, (1, 0), ((0, 1, 4),)),
    (4, (0, 0), ((1, 1, 1),)),
    (4, (0, 0), ((3, 3, 1),)),
    (0, (2, 2), ((3, 3, 1),)),
)
CAME = {0: (0, 0, 1), 1: (2, 2, 3), 2: (4, 4, 5), 3: (3, 3, 4)}


def hop_pairs(number, source, target, count):
    def at(segment, owner):
        return segment * count + owner

    def moves(sends):
        return [(at(a, p), at(b, p ^ step)) for a, b, step in sends for p in range(count)]

    last = count - 1
    back, rest = BESIDE_OWN[number]
    own = [(at(source, p), at(target, p)) for p in range(count)]
    own += moves(((target, source, back),) + rest)
    back, (leave, enter), rest = BESIDE_FACES[number]
    both = moves(((target, source, back),) + rest)
    down = both + [(at(source, p), at(target, p - 1)) for p in range(1, count)]
    down += [(at(leave, p), at(enter, p + 1)) for p in range(last)]
    down += [(at(source, 0), at(enter, 0)), (at(leave, last), at(target, last))]
    up = both + [(at(source, p), at(target, p + 1)) for p in range(last)]
    up += [(at(leave, p), at(enter, p - 1)) for p in range(1, count)]
    up += [(at(source, last), at(enter, last)), (at(leave, 0), at(target, 0))]
    return sorted(own), sorted(down), sorted(up)


def hop(number, source, target, count, low, high, own):
    straight, down, up = hop_pairs(number, source, target, count)
    return (
        lax.ppermute(own, AXES, straight),
        lax.ppermute(low, AXES, down),
        lax.ppermute(high, AXES, up),
    )


def halo_pairs(segments, count):
    last = count - 1
    one, two = [], []
    for even in range(0, segments, 2):
        a, b = even * count, (even + 1) * count
        one += [(a + p, a + p + 1) for p in range(last)] + [(a + last, b + last)]
        one += [(b + p, b + p - 1) for p in range(1, count)] + [(b, a)]
        two += [(a + p, a + p - 1) for p in range(1, count)] + [(a, b)]
        two += [(b + p, b + p + 1) for p in range(last)] + [(b + last, a + last)]
    return sorted(one), sorted(two)


def rms_scale(x32):
    return lax.rsqrt(jnp.mean(x32 * x32, axis=0, keepdims=True) + 1e-5)


def normalized(x):
    x32 = x.astype(F32)
    return (x32 * rms_scale(x32)).astype(BF16)


def stacked_lookup(low, own, high):
    first = jnp.concatenate([low, own[:, :LANES]], axis=1)
    second = jnp.concatenate([own[:, LANES:], high], axis=1)
    return jnp.concatenate([first, second], axis=0)


def one_hot(columns, missing):
    half = columns.shape[1]
    within = jnp.where(columns >= missing, -1, jnp.bitwise_and(columns, half - 1))
    places = lax.broadcasted_iota(jnp.int32, (half, half), 0).astype(F32).astype(BF16)
    within = within.astype(F32).astype(BF16)
    return jnp.where(places == within, jnp.ones((), BF16), jnp.zeros((), BF16))


def pick_rows(lookup, columns):
    channels, half = lookup.shape[0] // 2, lookup.shape[1]
    found = jnp.dot(lookup, one_hot(columns, 2 * half), preferred_element_type=F32)
    return jnp.where(columns >= half, found[channels:], found[:channels]).astype(BF16)


def silu_slope(z):
    sigmoid = jax.nn.sigmoid(z)
    return sigmoid * (1.0 + z * (1.0 - sigmoid))


def through_norm(x32, grad):
    inverse = rms_scale(x32)
    mean = jnp.mean(x32 * grad, axis=0, keepdims=True)
    return inverse * grad - x32 * (inverse * inverse * inverse) * mean


def even_segment():
    return jnp.where(lax.rem(lax.axis_index("segment"), 2) == 0, 1.0, 0.0).astype(F32) > 0.5


def prepare_kernel(features, live, x, one, two, landing, sem):
    copy = pltpu.make_async_copy(features, landing, sem)
    copy.start()
    copy.wait()
    rows = jnp.where(live[...] > 0.0, landing[...].astype(F32), jnp.zeros((), F32)).astype(BF16)
    x[...] = rows
    low, high = rows[:, :LANES], rows[:, LANES:]
    up = even_segment()
    one[...] = jnp.where(up, high, low)
    two[...] = jnp.where(up, low, high)


def load_kernel(weight_in, map_in, x, weight, row_map, coded, sems):
    copies = [
        pltpu.make_async_copy(weight_in, weight, sems.at[0]),
        pltpu.make_async_copy(map_in, row_map, sems.at[1]),
    ]
    for copy in copies:
        copy.start()
    for copy in copies:
        copy.wait()
    columns = row_map[...]
    small = jnp.where(columns > 256, 256 - columns, columns).astype(F32)
    spare = jnp.zeros((coded.shape[0] - columns.shape[0], columns.shape[1]), F32)
    coded[...] = jnp.concatenate([small, spare], axis=0).astype(BF16)


def gradient_kernel(cotangent, live, x, grad):
    grad[...] = jnp.where(live[...] > 0.0, cotangent[...].astype(F32), jnp.zeros((), F32))


def write_message(rows, below, own, low, high):
    own[: rows.shape[0], :] = rows
    low[: rows.shape[0], :] = rows[:, :LANES]
    high[: rows.shape[0], :] = rows[:, LANES:]
    own[rows.shape[0] :, :] = below
    low[rows.shape[0] :, :] = below[:, :LANES]
    high[rows.shape[0] :, :] = below[:, LANES:]


def forward_kernel(turn, *refs):
    (own_in, low_in, high_in, weight, row_map, coded, live, z_in, x_in, act_in) = refs[:10]
    (own, low, high, z, x, act) = refs[10:16]
    picked, results = refs[-1], refs[16:-1]
    segment = lax.axis_index("segment")
    offsets, channels = weight.shape[0], weight.shape[1]

    @pl.when(segment == turn)
    def _():
        rows = own_in[:channels, :]
        lookup = stacked_lookup(
            normalized(low_in[:channels, :]), normalized(rows), normalized(high_in[:channels, :])
        )
        for k in range(offsets):
            picked[k * channels : (k + 1) * channels, :] = pick_rows(lookup, row_map[k : k + 1, :])
        total = lax.dot_general(
            weight[...].reshape(offsets * channels, channels),
            picked[...],
            (((0,), (0,)), ((), ())),
            preferred_element_type=F32,
        )
        total = jnp.where(live[...] > 0.0, total, jnp.zeros((), F32))
        z[...] = total
        result = (rows.astype(F32) + total * jax.nn.sigmoid(total)).astype(BF16)
        write_message(result, coded[...], own, low, high)
        x[...] = rows
        act[...] = result
        for ref in results:
            ref[...] = result

    @pl.when(segment != turn)
    def _():
        z[...] = z_in[...]
        x[...] = x_in[...]
        act[...] = act_in[...]
        for ref in results:
            ref[...] = act_in[...]

    @pl.when(segment < turn)
    def _():
        write_message(act_in[...], coded[...], own, low, high)

    @pl.when(segment > turn)
    def _():
        write_message(x_in[...], coded[...], own, low, high)


def spread_body(dz, weight, row_map, masked, hot):
    offsets, channels = weight.shape[0], weight.shape[1]
    half = row_map.shape[1]
    for k in range(offsets):
        columns = row_map[k : k + 1, :]
        rows = jnp.dot(weight[k], dz, preferred_element_type=F32)
        upper = columns >= half
        zero = jnp.zeros((), F32)
        masked[:channels, k * half : (k + 1) * half] = jnp.where(upper, zero, rows).astype(BF16)
        masked[channels:, k * half : (k + 1) * half] = jnp.where(upper, rows, zero).astype(BF16)
        hot[:, k * half : (k + 1) * half] = one_hot(columns, 2 * half)
    return lax.dot_general(
        masked[...], hot[...], (((1,), (1,)), ((), ())), preferred_element_type=F32
    )


def face_terms(x, from_low, from_high):
    owner, count = lax.axis_index("space"), lax.axis_size("space")
    zero = jnp.zeros((), F32)
    lane = lax.broadcasted_iota(jnp.int32, (1, LANES), 1)
    has_low = lane + owner * LANES >= LANES
    has_high = lane + (owner + 1) * LANES < count * LANES
    low = jnp.where(has_low, from_low.astype(F32), zero)
    high = jnp.where(has_high, from_high.astype(F32), zero)
    return through_norm(x.astype(F32), jnp.concatenate([low, high], axis=1))


def slope_kernel(turn, segments, part_in, from_low, from_high, act, z, grad_in, dz_in, dz, grad):
    active = lax.axis_index("segment") == turn

    @pl.when(active)
    def _():
        if turn == segments - 1:
            total = grad_in[...]
        else:
            channels = act.shape[0]
            total = part_in[:channels, :].astype(F32) + face_terms(
                act[...], from_low[:channels, :], from_high[:channels, :]
            )
        grad[...] = total
        dz[...] = (total * silu_slope(z[...])).astype(BF16)

    @pl.when(jnp.logical_not(active))
    def _():
        dz[...] = dz_in[...]
        grad[...] = grad_in[...]


def spread_kernel(turn, dz, grad, x, act, weight, row_map, coded, part_in, low_in, high_in, *refs):
    (part, low, high), message, (masked, hot) = refs[:3], refs[3:-2], refs[-2:]
    active = lax.axis_index("segment") == turn

    @pl.when(active)
    def _():
        channels = x.shape[0]
        table = spread_body(dz[...], weight, row_map, masked, hot)
        own = jnp.concatenate([table[:channels, LANES:], table[channels:, :LANES]], axis=1)
        total = grad[...] + through_norm(x[...].astype(F32), own)
        part[...] = total
        to_low = table[:channels, :LANES].astype(BF16)
        to_high = table[channels:, LANES:].astype(BF16)
        low[...] = to_low
        high[...] = to_high
        if message:
            write_message(total.astype(BF16), coded[...], *message)
            message[1][:channels, :] = to_low
            message[2][:channels, :] = to_high

    @pl.when(jnp.logical_not(active))
    def _():
        part[...] = part_in[...]
        low[...] = low_in[...]
        high[...] = high_in[...]

    if message:
        segment = lax.axis_index("segment")

        @pl.when(segment == turn - 1)
        def _():
            write_message(act[...], coded[...], *message)

        @pl.when(jnp.logical_and(segment != turn, segment != turn - 1))
        def _():
            write_message(x[...], coded[...], *message)


def order_kernel(low, high, one, two):
    even = even_segment()
    one[...] = jnp.where(even, high[...], low[...])
    two[...] = jnp.where(even, low[...], high[...])


def finish_kernel(part, x, one, two, out):
    even = even_segment()
    from_low = jnp.where(even, one[...], two[...])
    from_high = jnp.where(even, two[...], one[...])
    out[...] = (part[...] + face_terms(x[...], from_low, from_high)).astype(BF16)


def decoded_columns(coded):
    coded = coded.astype(F32)
    return jnp.where(coded < 0.0, 256.0 - coded, coded).astype(jnp.int32)


def assemble_kernel(numbers, x, coded, *refs):
    received, out = refs[:-1], refs[-1]
    segment = lax.axis_index("segment")
    channels = x.shape[0]
    out[0, :channels, :] = x[...]
    out[0, channels:, :] = coded[...]
    for number in numbers:

        @pl.when(segment == number)
        def _(number=number):
            one, two, three = (received[3 * came : 3 * came + 3] for came in CAME[number])
            out[1] = one[0][...]
            out[2, :, :LANES] = two[1][...]
            out[2, :, LANES:] = two[2][...]
            out[3] = three[0][...]


def join_kernel(*refs):
    place = 0
    for ref in refs[:-1]:
        for i in range(ref.shape[0]):
            refs[-1][place] = ref[i]
            place += 1


def join(name, *stacks):
    shape = (sum(stack.shape[0] for stack in stacks),) + stacks[0].shape[1:]
    return call(join_kernel, name, struct(shape, stacks[0].dtype), *stacks)


def picked_body(channels, offsets, side, mine, other, picked, table):
    half, rows = mine.shape[0], mine.shape[2]
    owners = 2 * half
    me = lax.axis_index("space")
    for block in range(owners):
        source = mine if block < half else other
        table[block] = normalized(source[block % half][:channels])

    def place(owner):
        away = jnp.bitwise_xor(me, owner)
        return jnp.bitwise_and(away, 1) * half + jnp.right_shift(away, 1)

    for block in range(half):
        q = jnp.bitwise_xor(me, 2 * block + side)
        low = table[place(jnp.maximum(q - 1, 0))][:, LANES:]
        high = table[place(jnp.minimum(q + 1, owners - 1))][:, :LANES]
        lookup = stacked_lookup(low, table[side * half + block], high)
        columns = decoded_columns((other if side else mine)[block][channels:])
        for k in range(offsets):
            picked[k * channels : (k + 1) * channels, block * rows : (block + 1) * rows] = (
                pick_rows(lookup, columns[k : k + 1, :])
            )


def picked_kernel(channels, offsets, side, first, mine, other, *refs):
    picked, table = refs[-2:]
    segment = lax.axis_index("segment")

    @pl.when(segment == 0 if first else segment != 0)
    def _():
        picked_body(channels, offsets, side, mine, other, picked, table)


def weight_kernel(factor, picked, slopes, *refs):
    out = refs[-1]
    slopes = jnp.concatenate([slopes[i] for i in range(slopes.shape[0])], axis=1)
    offsets, channels = out.shape[0], out.shape[1]
    for k in range(offsets):
        total = lax.dot_general(
            picked[k * channels : (k + 1) * channels, :],
            slopes,
            (((1,), (1,)), ((), ())),
            preferred_element_type=F32,
        )
        for ref in refs[:-1]:
            total = total + ref[k]
        out[k] = factor * total


def lone_picked_kernel(low, own, high, row_map, picked):
    channels = own.shape[0]
    lookup = stacked_lookup(normalized(low[...]), normalized(own[...]), normalized(high[...]))
    for k in range(row_map.shape[0]):
        picked[k * channels : (k + 1) * channels, :] = pick_rows(lookup, row_map[k : k + 1, :])


def per_device(features, weights, row_map, block_count, cotangent):
    channels, rows = features.shape
    segments, count = lax.axis_size("segment"), lax.axis_size("space")
    offsets = row_map.shape[0]
    weight = weights[0]
    wide, face = (channels, rows), (channels, LANES)
    flops = 2 * offsets * channels * channels * rows
    live = (jnp.arange(rows, dtype=jnp.int32) < block_count[0] * LANES).astype(F32)[None, :]
    everyone = count == 8 and segments == 4

    current, one, two = call(
        prepare_kernel,
        "prepare",
        [struct(wide, BF16), struct(face, BF16), struct(face, BF16)],
        features,
        live,
        far=1,
        scratch=[pltpu.VMEM(wide, BF16), pltpu.SemaphoreType.DMA],
    )
    first, second = halo_pairs(segments, count)
    low, high = lax.ppermute(one, AXES, first), lax.ppermute(two, AXES, second)
    padded = -(-offsets // 16) * 16
    weight, row_map, coded = call(
        load_kernel,
        "load",
        [
            struct(weight.shape, BF16),
            struct(row_map.shape, jnp.int32),
            struct((padded, rows), BF16),
        ],
        weight,
        row_map,
        current,
        far=2,
        scratch=[pltpu.SemaphoreType.DMA((2,))],
    )
    cores = [(p, p ^ 1) for p in range(count)]
    block, half_block = (channels + padded, rows), (channels + padded, LANES)
    message = [struct(block, BF16), struct(half_block, BF16), struct(half_block, BF16)]
    received = []

    def assemble(name, numbers, *others):
        used = 1 + max(max(CAME[number]) for number in numbers)
        arrays = sum(received[:used], ())
        return call(
            functools.partial(assemble_kernel, numbers),
            name,
            struct((count // 2,) + block, BF16),
            x,
            coded,
            *after_all(arrays, others),
        )

    def pick(side, first, mine, other, *before):
        return call(
            functools.partial(picked_kernel, channels, offsets, side, first),
            f"picked{side}{'early' if first else 'late'}",
            struct((offsets * channels, count // 2 * rows), BF16),
            mine,
            other,
            *before,
            limit=24 << 20,
            scratch=[pltpu.VMEM((count, channels, rows), BF16)],
            flops=4 * flops,
            aliases={2: 0} if before else {},
        )

    z = jnp.zeros(wide, F32)
    x = act = own = current
    picked = []
    for turn in range(segments):
        outputs = call(
            functools.partial(forward_kernel, turn),
            f"forward{turn}",
            message
            + [struct(wide, F32), struct(wide, BF16), struct(wide, BF16)]
            + [struct(wide, BF16)] * (turn + 1 == segments),
            own,
            low,
            high,
            weight,
            row_map,
            coded,
            live,
            z,
            x,
            act,
            scratch=[pltpu.VMEM((offsets * channels, rows), BF16)],
            flops=flops,
        )
        sent, (z, x, act) = outputs[:3], outputs[3:6]
        acts = outputs[-1]
        if turn == 0:
            grad = call(gradient_kernel, "gradient", struct(wide, F32), cotangent, live, x)
        if turn + 1 < segments:
            if everyone and turn == segments - 2:
                early = assemble("early_rows", (0,), z)
                early_other = lax.ppermute(early, "space", cores)
            own, from_down, from_up = hop(
                len(received), turn, turn + 1, count, sent[1], sent[2], sent[0]
            )
            received.append((own, from_down, from_up))
            low, high = from_up, from_down

    dz = jnp.zeros(wide, BF16)
    part = grad
    out_low = out_high = jnp.zeros(face, BF16)
    for turn in reversed(range(segments)):
        own, from_high, from_low = received[-1]
        dz, grad = call(
            functools.partial(slope_kernel, turn, segments),
            f"slope{turn}",
            [struct(wide, BF16), struct(wide, F32)],
            own,
            from_low,
            from_high,
            act,
            z,
            grad,
            dz,
        )
        if turn == 0 and everyone:
            late = assemble("late_rows", tuple(range(1, segments)))
            slopes = [dz] + [
                lax.ppermute(dz, "space", [(p, p ^ (2 * m)) for p in range(count)])
                for m in range(1, count // 2)
            ]
            late_other = lax.ppermute(after(late, dz), "space", cores)
        part, out_low, out_high, *sent = call(
            functools.partial(spread_kernel, turn),
            f"spread{turn}",
            [struct(wide, F32), struct(face, BF16), struct(face, BF16)]
            + (message if turn > 0 else []),
            dz,
            grad,
            x,
            act,
            weight,
            row_map,
            coded,
            part,
            out_low,
            out_high,
            scratch=[
                pltpu.VMEM((2 * channels, offsets * rows), BF16),
                pltpu.VMEM((rows, offsets * rows), BF16),
            ],
            limit=16 << 20,
            flops=2 * flops,
        )
        if turn > 0:
            if everyone and len(picked) < 2:
                if not picked:
                    early_other = after(early_other, dz)
                picked.append(pick(len(picked), True, early, after(early_other, dz)))
                sent = after_all(sent, picked[-1:])
            received.append(
                hop(len(received), turn, turn - 1, count, sent[1], sent[2], sent[0])
            )

    one, two = call(
        order_kernel, "order", [struct(face, BF16), struct(face, BF16)], out_low, out_high
    )
    face_one, face_two = lax.ppermute(one, AXES, first), lax.ppermute(two, AXES, second)

    factor = 1.0 / math.sqrt(rows * count)
    shape = struct((offsets, channels, channels), F32)
    if everyone:
        picked = [pick(side, False, late, late_other, picked[side]) for side in range(2)]
        slopes = after_all(slopes, (face_one, face_two, picked[0]))
        slopes = join("slopes", *(block[None] for block in slopes))
        others = lax.ppermute(slopes, "space", cores)
        weight_grad = call(
            functools.partial(weight_kernel, 1.0),
            "weight_grad_mine",
            shape,
            picked[0],
            slopes,
            limit=24 << 20,
            flops=4 * flops,
        )
        face_one, face_two = lax.optimization_barrier((face_one, face_two, weight_grad))[:2]
        weight_grad = call(
            functools.partial(weight_kernel, factor),
            "weight_grad_all",
            shape,
            picked[1],
            others,
            weight_grad,
            limit=24 << 20,
            flops=4 * flops,
        )
    else:
        low = lax.ppermute(x[:, LANES:], "space", [(p, p + 1) for p in range(count - 1)])
        high = lax.ppermute(x[:, :LANES], "space", [(p, p - 1) for p in range(1, count)])
        picked = call(
            lone_picked_kernel,
            "lone_picked",
            struct((offsets * channels, rows), BF16),
            low,
            x,
            high,
            row_map,
        )
        weight_grad = call(
            functools.partial(weight_kernel, factor), "weight_grad", shape, picked, dz[None]
        )
        weight_grad = lax.psum(weight_grad, "space")
    grad_in = call(finish_kernel, "finish", struct(wide, BF16), part, x, face_one, face_two)
    return acts[None], grad_in[None], weight_grad[None]


def solution(mesh):
    placed = (
        P(None, "space"),
        P("segment", None, None, None),
        P(None, "space"),
        P("space"),
        P(None, "space"),
    )
    return jax.shard_map(
        per_device,
        mesh=mesh,
        in_specs=placed,
        out_specs=(
            P("segment", None, "space"),
            P("segment", None, "space"),
            P("segment", None, None, None),
        ),
        check_vma=False,
    )
```

```python
import functools
import math

import jax
import jax.numpy as jnp
from jax import lax
from jax.experimental import pallas as pl
from jax.experimental.pallas import tpu as pltpu
from jax.sharding import PartitionSpec as P

AXES = ("segment", "space")
BF16 = jnp.bfloat16
F32 = jnp.float32
LANES = 128
VMEM = pl.BlockSpec(memory_space=pltpu.VMEM)
HBM = pl.BlockSpec(memory_space=pltpu.HBM)


def call(body, name, out_shape, *args, limit=8 << 20, scratch=(), flops=0, far=0, aliases=None):
    return pl.pallas_call(
        body,
        name=name,
        out_shape=out_shape,
        in_specs=[HBM] * far + [VMEM] * (len(args) - far),
        out_specs=jax.tree.map(lambda _: VMEM, out_shape),
        scratch_shapes=list(scratch),
        input_output_aliases=aliases or {},
        compiler_params=pltpu.CompilerParams(vmem_limit_bytes=limit),
        cost_estimate=pl.CostEstimate(flops=flops, bytes_accessed=0, transcendentals=0),
    )(*args)


def after(value, *others):
    return lax.optimization_barrier((value,) + others)[0]


def after_all(values, others):
    return lax.optimization_barrier((*values, *others))[: len(values)]


def struct(shape, dtype):
    return jax.ShapeDtypeStruct(shape, dtype)


BESIDE_OWN = (
    (2, ((2, 2, 1), (3, 3, 1))),
    (0, ((3, 0, 6), (0, 3, 0))),
    (0, ((0, 1, 2), (1, 0, 0))),
    (2, ((1, 1, 6), (0, 0, 1))),
    (2, ((3, 3, 6), (0, 0, 1))),
    (0, ((2, 2, 6), (3, 3, 1))),
)
BESIDE_FACES = (
    (4, (3, 3), ((2, 2, 1),)),
    (0, (3, 3), ((0, 0, 1),)),
    (0, (1, 0), ((0, 1, 4),)),
    (4, (0, 0), ((1, 1, 1),)),
    (4, (3, 3), ((0, 0, 1),)),
    (0, (3, 3), ((2, 2, 1),)),
)
CAME = {0: (0, 0, 1), 1: (2, 2, 3), 2: (4, 4, 5), 3: (3, 3, 4)}


def hop_pairs(number, source, target, count):
    def at(segment, owner):
        return segment * count + owner

    def moves(sends):
        return [(at(a, p), at(b, p ^ step)) for a, b, step in sends for p in range(count)]

    last = count - 1
    back, rest = BESIDE_OWN[number]
    own = [(at(source, p), at(target, p)) for p in range(count)]
    own += moves(((target, source, back),) + rest)
    back, (leave, enter), rest = BESIDE_FACES[number]
    both = moves(((target, source, back),) + rest)
    down = both + [(at(source, p), at(target, p - 1)) for p in range(1, count)]
    down += [(at(leave, p), at(enter, p + 1)) for p in range(last)]
    down += [(at(source, 0), at(enter, 0)), (at(leave, last), at(target, last))]
    up = both + [(at(source, p), at(target, p + 1)) for p in range(last)]
    up += [(at(leave, p), at(enter, p - 1)) for p in range(1, count)]
    up += [(at(source, last), at(enter, last)), (at(leave, 0), at(target, 0))]
    return sorted(own), sorted(down), sorted(up)


def hop(number, source, target, count, low, high, own):
    straight, down, up = hop_pairs(number, source, target, count)
    return (
        lax.ppermute(own, AXES, straight),
        lax.ppermute(low, AXES, down),
        lax.ppermute(high, AXES, up),
    )


def halo_pairs(segments, count):
    last = count - 1
    one, two = [], []
    for even in range(0, segments, 2):
        a, b = even * count, (even + 1) * count
        one += [(a + p, a + p + 1) for p in range(last)] + [(a + last, b + last)]
        one += [(b + p, b + p - 1) for p in range(1, count)] + [(b, a)]
        two += [(a + p, a + p - 1) for p in range(1, count)] + [(a, b)]
        two += [(b + p, b + p + 1) for p in range(last)] + [(b + last, a + last)]
    return sorted(one), sorted(two)


def rms_scale(x32):
    return lax.rsqrt(jnp.mean(x32 * x32, axis=0, keepdims=True) + 1e-5)


def normalized(x):
    x32 = x.astype(F32)
    return (x32 * rms_scale(x32)).astype(BF16)


def stacked_lookup(low, own, high):
    first = jnp.concatenate([low, own[:, :LANES]], axis=1)
    second = jnp.concatenate([own[:, LANES:], high], axis=1)
    return jnp.concatenate([first, second], axis=0)


def one_hot(columns, missing):
    half = columns.shape[1]
    within = jnp.where(columns >= missing, -1, jnp.bitwise_and(columns, half - 1))
    places = lax.broadcasted_iota(jnp.int32, (half, half), 0).astype(F32).astype(BF16)
    within = within.astype(F32).astype(BF16)
    return jnp.where(places == within, jnp.ones((), BF16), jnp.zeros((), BF16))


def pick_rows(lookup, columns):
    channels, half = lookup.shape[0] // 2, lookup.shape[1]
    found = jnp.dot(lookup, one_hot(columns, 2 * half), preferred_element_type=F32)
    return jnp.where(columns >= half, found[channels:], found[:channels]).astype(BF16)


def silu_slope(z):
    sigmoid = jax.nn.sigmoid(z)
    return sigmoid * (1.0 + z * (1.0 - sigmoid))


def through_norm(x32, grad):
    inverse = rms_scale(x32)
    mean = jnp.mean(x32 * grad, axis=0, keepdims=True)
    return inverse * grad - x32 * (inverse * inverse * inverse) * mean


def even_segment():
    return jnp.where(lax.rem(lax.axis_index("segment"), 2) == 0, 1.0, 0.0).astype(F32) > 0.5


def prepare_kernel(features, live, x, one, two, landing, sem):
    copy = pltpu.make_async_copy(features, landing, sem)
    copy.start()
    copy.wait()
    rows = jnp.where(live[...] > 0.0, landing[...].astype(F32), jnp.zeros((), F32)).astype(BF16)
    x[...] = rows
    low, high = rows[:, :LANES], rows[:, LANES:]
    up = even_segment()
    one[...] = jnp.where(up, high, low)
    two[...] = jnp.where(up, low, high)


def load_kernel(weight_in, map_in, x, weight, row_map, coded, sems):
    copies = [
        pltpu.make_async_copy(weight_in, weight, sems.at[0]),
        pltpu.make_async_copy(map_in, row_map, sems.at[1]),
    ]
    for copy in copies:
        copy.start()
    for copy in copies:
        copy.wait()
    columns = row_map[...]
    small = jnp.where(columns > 256, 256 - columns, columns).astype(F32)
    spare = jnp.zeros((coded.shape[0] - columns.shape[0], columns.shape[1]), F32)
    coded[...] = jnp.concatenate([small, spare], axis=0).astype(BF16)


def gradient_kernel(cotangent, live, x, grad):
    grad[...] = jnp.where(live[...] > 0.0, cotangent[...].astype(F32), jnp.zeros((), F32))


def write_message(rows, below, own, low, high):
    own[: rows.shape[0], :] = rows
    low[: rows.shape[0], :] = rows[:, :LANES]
    high[: rows.shape[0], :] = rows[:, LANES:]
    own[rows.shape[0] :, :] = below
    low[rows.shape[0] :, :] = below[:, :LANES]
    high[rows.shape[0] :, :] = below[:, LANES:]


def forward_kernel(turn, *refs):
    (own_in, low_in, high_in, weight, row_map, coded, live, z_in, x_in, act_in) = refs[:10]
    (own, low, high, z, x, act) = refs[10:16]
    picked, results = refs[-1], refs[16:-1]
    segment = lax.axis_index("segment")
    offsets, channels = weight.shape[0], weight.shape[1]

    @pl.when(segment == turn)
    def _():
        rows = own_in[:channels, :]
        lookup = stacked_lookup(
            normalized(low_in[:channels, :]), normalized(rows), normalized(high_in[:channels, :])
        )
        for k in range(offsets):
            picked[k * channels : (k + 1) * channels, :] = pick_rows(lookup, row_map[k : k + 1, :])
        total = lax.dot_general(
            weight[...].reshape(offsets * channels, channels),
            picked[...],
            (((0,), (0,)), ((), ())),
            preferred_element_type=F32,
        )
        total = jnp.where(live[...] > 0.0, total, jnp.zeros((), F32))
        z[...] = total
        result = (rows.astype(F32) + total * jax.nn.sigmoid(total)).astype(BF16)
        write_message(result, coded[...], own, low, high)
        x[...] = rows
        act[...] = result
        for ref in results:
            ref[...] = result

    @pl.when(segment != turn)
    def _():
        z[...] = z_in[...]
        x[...] = x_in[...]
        act[...] = act_in[...]
        for ref in results:
            ref[...] = act_in[...]

    @pl.when(segment < turn)
    def _():
        write_message(act_in[...], coded[...], own, low, high)

    @pl.when(segment > turn)
    def _():
        write_message(x_in[...], coded[...], own, low, high)


def spread_body(dz, weight, row_map, masked, hot):
    offsets, channels = weight.shape[0], weight.shape[1]
    half = row_map.shape[1]
    for k in range(offsets):
        columns = row_map[k : k + 1, :]
        rows = jnp.dot(weight[k], dz, preferred_element_type=F32)
        upper = columns >= half
        zero = jnp.zeros((), F32)
        masked[:channels, k * half : (k + 1) * half] = jnp.where(upper, zero, rows).astype(BF16)
        masked[channels:, k * half : (k + 1) * half] = jnp.where(upper, rows, zero).astype(BF16)
        hot[:, k * half : (k + 1) * half] = one_hot(columns, 2 * half)
    return lax.dot_general(
        masked[...], hot[...], (((1,), (1,)), ((), ())), preferred_element_type=F32
    )


def face_terms(x, from_low, from_high):
    owner, count = lax.axis_index("space"), lax.axis_size("space")
    zero = jnp.zeros((), F32)
    lane = lax.broadcasted_iota(jnp.int32, (1, LANES), 1)
    has_low = lane + owner * LANES >= LANES
    has_high = lane + (owner + 1) * LANES < count * LANES
    low = jnp.where(has_low, from_low.astype(F32), zero)
    high = jnp.where(has_high, from_high.astype(F32), zero)
    return through_norm(x.astype(F32), jnp.concatenate([low, high], axis=1))


def slope_kernel(turn, segments, part_in, from_low, from_high, act, z, grad_in, dz_in, dz, grad):
    active = lax.axis_index("segment") == turn

    @pl.when(active)
    def _():
        if turn == segments - 1:
            total = grad_in[...]
        else:
            channels = act.shape[0]
            total = part_in[:channels, :].astype(F32) + face_terms(
                act[...], from_low[:channels, :], from_high[:channels, :]
            )
        grad[...] = total
        dz[...] = (total * silu_slope(z[...])).astype(BF16)

    @pl.when(jnp.logical_not(active))
    def _():
        dz[...] = dz_in[...]
        grad[...] = grad_in[...]


def spread_kernel(turn, dz, grad, x, act, weight, row_map, coded, part_in, low_in, high_in, *refs):
    (part, low, high), message, (masked, hot) = refs[:3], refs[3:-2], refs[-2:]
    active = lax.axis_index("segment") == turn

    @pl.when(active)
    def _():
        channels = x.shape[0]
        table = spread_body(dz[...], weight, row_map, masked, hot)
        own = jnp.concatenate([table[:channels, LANES:], table[channels:, :LANES]], axis=1)
        total = grad[...] + through_norm(x[...].astype(F32), own)
        part[...] = total
        to_low = table[:channels, :LANES].astype(BF16)
        to_high = table[channels:, LANES:].astype(BF16)
        low[...] = to_low
        high[...] = to_high
        if message:
            write_message(total.astype(BF16), coded[...], *message)
            message[1][:channels, :] = to_low
            message[2][:channels, :] = to_high

    @pl.when(jnp.logical_not(active))
    def _():
        part[...] = part_in[...]
        low[...] = low_in[...]
        high[...] = high_in[...]

    if message:
        segment = lax.axis_index("segment")

        @pl.when(segment == turn - 1)
        def _():
            write_message(act[...], coded[...], *message)

        @pl.when(jnp.logical_and(segment != turn, segment != turn - 1))
        def _():
            write_message(x[...], coded[...], *message)


def order_kernel(low, high, one, two):
    even = even_segment()
    one[...] = jnp.where(even, high[...], low[...])
    two[...] = jnp.where(even, low[...], high[...])


def finish_kernel(part, x, one, two, out):
    even = even_segment()
    from_low = jnp.where(even, one[...], two[...])
    from_high = jnp.where(even, two[...], one[...])
    out[...] = (part[...] + face_terms(x[...], from_low, from_high)).astype(BF16)


def decoded_columns(coded):
    coded = coded.astype(F32)
    return jnp.where(coded < 0.0, 256.0 - coded, coded).astype(jnp.int32)


def assemble_kernel(numbers, x, coded, *refs):
    received, out = refs[:-1], refs[-1]
    segment = lax.axis_index("segment")
    channels = x.shape[0]
    out[0, :channels, :] = x[...]
    out[0, channels:, :] = coded[...]
    for number in numbers:

        @pl.when(segment == number)
        def _(number=number):
            one, two, three = (received[3 * came : 3 * came + 3] for came in CAME[number])
            out[1] = one[0][...]
            out[2, :, :LANES] = two[1][...]
            out[2, :, LANES:] = two[2][...]
            out[3] = three[0][...]


def join_kernel(*refs):
    place = 0
    for ref in refs[:-1]:
        for i in range(ref.shape[0]):
            refs[-1][place] = ref[i]
            place += 1


def join(name, *stacks):
    shape = (sum(stack.shape[0] for stack in stacks),) + stacks[0].shape[1:]
    return call(join_kernel, name, struct(shape, stacks[0].dtype), *stacks)


def picked_body(channels, offsets, side, mine, other, picked, table):
    half, rows = mine.shape[0], mine.shape[2]
    owners = 2 * half
    me = lax.axis_index("space")
    for block in range(owners):
        source = mine if block < half else other
        table[block] = normalized(source[block % half][:channels])

    def place(owner):
        away = jnp.bitwise_xor(me, owner)
        return jnp.bitwise_and(away, 1) * half + jnp.right_shift(away, 1)

    for block in range(half):
        q = jnp.bitwise_xor(me, 2 * block + side)
        low = table[place(jnp.maximum(q - 1, 0))][:, LANES:]
        high = table[place(jnp.minimum(q + 1, owners - 1))][:, :LANES]
        lookup = stacked_lookup(low, table[side * half + block], high)
        columns = decoded_columns((other if side else mine)[block][channels:])
        for k in range(offsets):
            picked[k * channels : (k + 1) * channels, block * rows : (block + 1) * rows] = (
                pick_rows(lookup, columns[k : k + 1, :])
            )


def picked_kernel(channels, offsets, side, first, mine, other, *refs):
    picked, table = refs[-2:]
    segment = lax.axis_index("segment")

    @pl.when(segment == 0 if first else segment != 0)
    def _():
        picked_body(channels, offsets, side, mine, other, picked, table)


def weight_kernel(factor, picked, slopes, *refs):
    out = refs[-1]
    slopes = jnp.concatenate([slopes[i] for i in range(slopes.shape[0])], axis=1)
    offsets, channels = out.shape[0], out.shape[1]
    for k in range(offsets):
        total = lax.dot_general(
            picked[k * channels : (k + 1) * channels, :],
            slopes,
            (((1,), (1,)), ((), ())),
            preferred_element_type=F32,
        )
        for ref in refs[:-1]:
            total = total + ref[k]
        out[k] = factor * total


def last_kernel(factor, picked, slopes, before, part, x, one, two, weight_grad, grad_in):
    finish_kernel(part, x, one, two, grad_in)
    weight_kernel(factor, picked, slopes, before, weight_grad)


def lone_picked_kernel(low, own, high, row_map, picked):
    channels = own.shape[0]
    lookup = stacked_lookup(normalized(low[...]), normalized(own[...]), normalized(high[...]))
    for k in range(row_map.shape[0]):
        picked[k * channels : (k + 1) * channels, :] = pick_rows(lookup, row_map[k : k + 1, :])


def per_device(features, weights, row_map, block_count, cotangent):
    channels, rows = features.shape
    segments, count = lax.axis_size("segment"), lax.axis_size("space")
    offsets = row_map.shape[0]
    weight = weights[0]
    wide, face = (channels, rows), (channels, LANES)
    flops = 2 * offsets * channels * channels * rows
    live = (jnp.arange(rows, dtype=jnp.int32) < block_count[0] * LANES).astype(F32)[None, :]
    everyone = count == 8 and segments == 4

    current, one, two = call(
        prepare_kernel,
        "prepare",
        [struct(wide, BF16), struct(face, BF16), struct(face, BF16)],
        features,
        live,
        far=1,
        scratch=[pltpu.VMEM(wide, BF16), pltpu.SemaphoreType.DMA],
    )
    first, second = halo_pairs(segments, count)
    low, high = lax.ppermute(one, AXES, first), lax.ppermute(two, AXES, second)
    padded = -(-offsets // 16) * 16
    weight, row_map, coded = call(
        load_kernel,
        "load",
        [
            struct(weight.shape, BF16),
            struct(row_map.shape, jnp.int32),
            struct((padded, rows), BF16),
        ],
        weight,
        row_map,
        current,
        far=2,
        scratch=[pltpu.SemaphoreType.DMA((2,))],
    )
    cores = [(p, p ^ 1) for p in range(count)]
    block, half_block = (channels + padded, rows), (channels + padded, LANES)
    message = [struct(block, BF16), struct(half_block, BF16), struct(half_block, BF16)]
    received = []

    def assemble(name, numbers, *others):
        used = 1 + max(max(CAME[number]) for number in numbers)
        arrays = sum(received[:used], ())
        return call(
            functools.partial(assemble_kernel, numbers),
            name,
            struct((count // 2,) + block, BF16),
            x,
            coded,
            *after_all(arrays, others),
        )

    def pick(side, first, mine, other, *before):
        return call(
            functools.partial(picked_kernel, channels, offsets, side, first),
            f"picked{side}{'early' if first else 'late'}",
            struct((offsets * channels, count // 2 * rows), BF16),
            mine,
            other,
            *before,
            limit=24 << 20,
            scratch=[pltpu.VMEM((count, channels, rows), BF16)],
            flops=4 * flops,
            aliases={2: 0} if before else {},
        )

    z = jnp.zeros(wide, F32)
    x = act = own = current
    picked = []
    for turn in range(segments):
        outputs = call(
            functools.partial(forward_kernel, turn),
            f"forward{turn}",
            message
            + [struct(wide, F32), struct(wide, BF16), struct(wide, BF16)]
            + [struct(wide, BF16)] * (turn + 1 == segments),
            own,
            low,
            high,
            weight,
            row_map,
            coded,
            live,
            z,
            x,
            act,
            scratch=[pltpu.VMEM((offsets * channels, rows), BF16)],
            flops=flops,
        )
        sent, (z, x, act) = outputs[:3], outputs[3:6]
        acts = outputs[-1]
        if turn == 0:
            grad = call(gradient_kernel, "gradient", struct(wide, F32), cotangent, live, x)
        if turn + 1 < segments:
            if everyone and turn == segments - 2:
                early = assemble("early_rows", (0,), z)
                early_other = lax.ppermute(early, "space", cores)
            own, from_down, from_up = hop(
                len(received), turn, turn + 1, count, sent[1], sent[2], sent[0]
            )
            received.append((own, from_down, from_up))
            low, high = from_up, from_down

    dz = jnp.zeros(wide, BF16)
    part = grad
    out_low = out_high = jnp.zeros(face, BF16)
    for turn in reversed(range(segments)):
        own, from_high, from_low = received[-1]
        dz, grad = call(
            functools.partial(slope_kernel, turn, segments),
            f"slope{turn}",
            [struct(wide, BF16), struct(wide, F32)],
            own,
            from_low,
            from_high,
            act,
            z,
            grad,
            dz,
        )
        if turn == 0 and everyone:
            late = assemble("late_rows", tuple(range(1, segments)))
            slopes = [dz] + [
                lax.ppermute(dz, "space", [(p, p ^ (2 * m)) for p in range(count)])
                for m in range(1, count // 2)
            ]
            late_other = lax.ppermute(after(late, dz), "space", cores)
        part, out_low, out_high, *sent = call(
            functools.partial(spread_kernel, turn),
            f"spread{turn}",
            [struct(wide, F32), struct(face, BF16), struct(face, BF16)]
            + (message if turn > 0 else []),
            dz,
            grad,
            x,
            act,
            weight,
            row_map,
            coded,
            part,
            out_low,
            out_high,
            scratch=[
                pltpu.VMEM((2 * channels, offsets * rows), BF16),
                pltpu.VMEM((rows, offsets * rows), BF16),
            ],
            limit=16 << 20,
            flops=2 * flops,
        )
        if turn > 0:
            if everyone and len(picked) < 2:
                if not picked:
                    early_other = after(early_other, dz)
                picked.append(pick(len(picked), True, early, after(early_other, dz)))
                sent = after_all(sent, picked[-1:])
            received.append(
                hop(len(received), turn, turn - 1, count, sent[1], sent[2], sent[0])
            )

    one, two = call(
        order_kernel, "order", [struct(face, BF16), struct(face, BF16)], out_low, out_high
    )
    face_one, face_two = lax.ppermute(one, AXES, first), lax.ppermute(two, AXES, second)

    factor = 1.0 / math.sqrt(rows * count)
    shape = struct((offsets, channels, channels), F32)
    if everyone:
        picked = [pick(side, False, late, late_other, picked[side]) for side in range(2)]
        slopes = after_all(slopes, (one, two, picked[0]))
        slopes = join("slopes", *(block[None] for block in slopes))
        others = lax.ppermute(slopes, "space", cores)
        weight_grad = call(
            functools.partial(weight_kernel, 1.0),
            "weight_grad_mine",
            shape,
            picked[0],
            slopes,
            limit=24 << 20,
            flops=4 * flops,
        )
        face_one, face_two = after_all((face_one, face_two), (weight_grad, picked[1]))
        weight_grad, grad_in = call(
            functools.partial(last_kernel, factor),
            "last",
            [shape, struct(wide, BF16)],
            picked[1],
            others,
            weight_grad,
            part,
            x,
            face_one,
            face_two,
            limit=24 << 20,
            flops=4 * flops,
        )
    else:
        low = lax.ppermute(x[:, LANES:], "space", [(p, p + 1) for p in range(count - 1)])
        high = lax.ppermute(x[:, :LANES], "space", [(p, p - 1) for p in range(1, count)])
        picked = call(
            lone_picked_kernel,
            "lone_picked",
            struct((offsets * channels, rows), BF16),
            low,
            x,
            high,
            row_map,
        )
        weight_grad = call(
            functools.partial(weight_kernel, factor), "weight_grad", shape, picked, dz[None]
        )
        weight_grad = lax.psum(weight_grad, "space")
        grad_in = call(finish_kernel, "finish", struct(wide, BF16), part, x, face_one, face_two)
    return acts[None], grad_in[None], weight_grad[None]


def solution(mesh):
    placed = (
        P(None, "space"),
        P("segment", None, None, None),
        P(None, "space"),
        P("space"),
        P(None, "space"),
    )
    return jax.shard_map(
        per_device,
        mesh=mesh,
        in_specs=placed,
        out_specs=(
            P("segment", None, "space"),
            P("segment", None, "space"),
            P("segment", None, None, None),
        ),
        check_vma=False,
    )
```

```python
import functools
import math

import jax
import jax.numpy as jnp
from jax import lax
from jax.experimental import pallas as pl
from jax.experimental.pallas import tpu as pltpu
from jax.sharding import PartitionSpec as P

AXES = ("segment", "space")
BF16 = jnp.bfloat16
F32 = jnp.float32
LANES = 128
VMEM = pl.BlockSpec(memory_space=pltpu.VMEM)
HBM = pl.BlockSpec(memory_space=pltpu.HBM)


def call(body, name, out_shape, *args, limit=8 << 20, scratch=(), flops=0, far=0, aliases=None):
    return pl.pallas_call(
        body,
        name=name,
        out_shape=out_shape,
        in_specs=[HBM] * far + [VMEM] * (len(args) - far),
        out_specs=jax.tree.map(lambda _: VMEM, out_shape),
        scratch_shapes=list(scratch),
        input_output_aliases=aliases or {},
        compiler_params=pltpu.CompilerParams(vmem_limit_bytes=limit),
        cost_estimate=pl.CostEstimate(flops=flops, bytes_accessed=0, transcendentals=0),
    )(*args)


def after(value, *others):
    return lax.optimization_barrier((value,) + others)[0]


def after_all(values, others):
    return lax.optimization_barrier((*values, *others))[: len(values)]


def struct(shape, dtype):
    return jax.ShapeDtypeStruct(shape, dtype)


BESIDE_OWN = (
    (2, ((2, 2, 1), (3, 3, 1))),
    (0, ((3, 0, 6), (0, 3, 0))),
    (0, ((0, 1, 2), (1, 0, 0))),
    (2, ((1, 1, 6), (0, 0, 1))),
    (2, ((3, 3, 6), (0, 0, 1))),
    (0, ((2, 2, 6), (3, 3, 1))),
)
BESIDE_FACES = (
    (4, (3, 3), ((2, 2, 1),)),
    (0, (3, 3), ((0, 0, 1),)),
    (0, (1, 0), ((0, 1, 4),)),
    (4, (0, 0), ((1, 1, 1),)),
    (4, (3, 3), ((0, 0, 1),)),
    (0, (3, 3), ((2, 2, 1),)),
)
CAME = {0: (0, 0, 1), 1: (2, 2, 3), 2: (4, 4, 5), 3: (3, 3, 4)}


def hop_pairs(number, source, target, count):
    def at(segment, owner):
        return segment * count + owner

    def moves(sends):
        return [(at(a, p), at(b, p ^ step)) for a, b, step in sends for p in range(count)]

    last = count - 1
    back, rest = BESIDE_OWN[number]
    own = [(at(source, p), at(target, p)) for p in range(count)]
    own += moves(((target, source, back),) + rest)
    back, (leave, enter), rest = BESIDE_FACES[number]
    both = moves(((target, source, back),) + rest)
    down = both + [(at(source, p), at(target, p - 1)) for p in range(1, count)]
    down += [(at(leave, p), at(enter, p + 1)) for p in range(last)]
    down += [(at(source, 0), at(enter, 0)), (at(leave, last), at(target, last))]
    up = both + [(at(source, p), at(target, p + 1)) for p in range(last)]
    up += [(at(leave, p), at(enter, p - 1)) for p in range(1, count)]
    up += [(at(source, last), at(enter, last)), (at(leave, 0), at(target, 0))]
    return sorted(own), sorted(down), sorted(up)


def hop(number, source, target, count, low, high, own):
    straight, down, up = hop_pairs(number, source, target, count)
    return (
        lax.ppermute(own, AXES, straight),
        lax.ppermute(low, AXES, down),
        lax.ppermute(high, AXES, up),
    )


def halo_pairs(segments, count):
    last = count - 1
    one, two = [], []
    for even in range(0, segments, 2):
        a, b = even * count, (even + 1) * count
        one += [(a + p, a + p + 1) for p in range(last)] + [(a + last, b + last)]
        one += [(b + p, b + p - 1) for p in range(1, count)] + [(b, a)]
        two += [(a + p, a + p - 1) for p in range(1, count)] + [(a, b)]
        two += [(b + p, b + p + 1) for p in range(last)] + [(b + last, a + last)]
    return sorted(one), sorted(two)


def rms_scale(x32):
    return lax.rsqrt(jnp.mean(x32 * x32, axis=0, keepdims=True) + 1e-5)


def normalized(x):
    x32 = x.astype(F32)
    return (x32 * rms_scale(x32)).astype(BF16)


def stacked_lookup(low, own, high):
    first = jnp.concatenate([low, own[:, :LANES]], axis=1)
    second = jnp.concatenate([own[:, LANES:], high], axis=1)
    return jnp.concatenate([first, second], axis=0)


def one_hot(columns, missing):
    half = columns.shape[1]
    within = jnp.where(columns >= missing, -1, jnp.bitwise_and(columns, half - 1))
    places = lax.broadcasted_iota(jnp.int32, (half, half), 0).astype(F32).astype(BF16)
    within = within.astype(F32).astype(BF16)
    return jnp.where(places == within, jnp.ones((), BF16), jnp.zeros((), BF16))


def pick_rows(lookup, columns):
    channels, half = lookup.shape[0] // 2, lookup.shape[1]
    found = jnp.dot(lookup, one_hot(columns, 2 * half), preferred_element_type=F32)
    return jnp.where(columns >= half, found[channels:], found[:channels]).astype(BF16)


def gather_rows(blocks, columns):
    halves = []
    for first in range(0, columns.shape[1], LANES):
        wanted = columns[:, first : first + LANES]
        lane = jnp.broadcast_to(jnp.bitwise_and(wanted, LANES - 1), blocks[0].shape)
        found = jnp.zeros((), F32)
        for place in reversed(range(len(blocks))):
            there = jnp.take_along_axis(blocks[place], lane, axis=1, mode="promise_in_bounds")
            found = jnp.where(wanted < (place + 1) * LANES, there, found)
        halves.append(found)
    return jnp.concatenate(halves, axis=1).astype(BF16)


def pick_all(lookup, columns, store, share=0):
    channels, offsets = lookup.shape[0] // 2, columns.shape[0]
    wide = lookup.astype(F32)
    blocks = [
        wide[half : half + channels, lane : lane + LANES]
        for half in (0, channels)
        for lane in (0, LANES)
    ]
    for k in range(offsets):
        row = columns[k : k + 1, :]
        gathered = (k * share) // offsets != ((k + 1) * share) // offsets
        store(k, gather_rows(blocks, row) if gathered else pick_rows(lookup, row))


def silu_slope(z):
    sigmoid = jax.nn.sigmoid(z)
    return sigmoid * (1.0 + z * (1.0 - sigmoid))


def through_norm(x32, grad):
    inverse = rms_scale(x32)
    mean = jnp.mean(x32 * grad, axis=0, keepdims=True)
    return inverse * grad - x32 * (inverse * inverse * inverse) * mean


def even_segment():
    return jnp.where(lax.rem(lax.axis_index("segment"), 2) == 0, 1.0, 0.0).astype(F32) > 0.5


def prepare_kernel(features, live, x, one, two, landing, sem):
    copy = pltpu.make_async_copy(features, landing, sem)
    copy.start()
    copy.wait()
    rows = jnp.where(live[...] > 0.0, landing[...].astype(F32), jnp.zeros((), F32)).astype(BF16)
    x[...] = rows
    low, high = rows[:, :LANES], rows[:, LANES:]
    up = even_segment()
    one[...] = jnp.where(up, high, low)
    two[...] = jnp.where(up, low, high)


def load_kernel(weight_in, map_in, x, weight, row_map, coded, sems):
    copies = [
        pltpu.make_async_copy(weight_in, weight, sems.at[0]),
        pltpu.make_async_copy(map_in, row_map, sems.at[1]),
    ]
    for copy in copies:
        copy.start()
    for copy in copies:
        copy.wait()
    columns = row_map[...]
    small = jnp.where(columns > 256, 256 - columns, columns).astype(F32)
    spare = jnp.zeros((coded.shape[0] - columns.shape[0], columns.shape[1]), F32)
    coded[...] = jnp.concatenate([small, spare], axis=0).astype(BF16)


def gradient_kernel(cotangent, live, x, grad):
    grad[...] = jnp.where(live[...] > 0.0, cotangent[...].astype(F32), jnp.zeros((), F32))


def write_message(rows, below, own, low, high):
    own[: rows.shape[0], :] = rows
    low[: rows.shape[0], :] = rows[:, :LANES]
    high[: rows.shape[0], :] = rows[:, LANES:]
    own[rows.shape[0] :, :] = below
    low[rows.shape[0] :, :] = below[:, :LANES]
    high[rows.shape[0] :, :] = below[:, LANES:]


def forward_kernel(turn, *refs):
    (own_in, low_in, high_in, weight, row_map, coded, live, z_in, x_in, act_in) = refs[:10]
    (own, low, high, z, x, act) = refs[10:16]
    picked, results = refs[-1], refs[16:-1]
    segment = lax.axis_index("segment")
    offsets, channels = weight.shape[0], weight.shape[1]

    @pl.when(segment == turn)
    def _():
        rows = own_in[:channels, :]
        lookup = stacked_lookup(
            normalized(low_in[:channels, :]), normalized(rows), normalized(high_in[:channels, :])
        )

        def store(k, rows_of_k):
            picked[k * channels : (k + 1) * channels, :] = rows_of_k

        pick_all(lookup, row_map[...], store, share=8)
        total = lax.dot_general(
            weight[...].reshape(offsets * channels, channels),
            picked[...],
            (((0,), (0,)), ((), ())),
            preferred_element_type=F32,
        )
        total = jnp.where(live[...] > 0.0, total, jnp.zeros((), F32))
        z[...] = total
        result = (rows.astype(F32) + total * jax.nn.sigmoid(total)).astype(BF16)
        write_message(result, coded[...], own, low, high)
        x[...] = rows
        act[...] = result
        for ref in results:
            ref[...] = result

    @pl.when(segment != turn)
    def _():
        z[...] = z_in[...]
        x[...] = x_in[...]
        act[...] = act_in[...]
        for ref in results:
            ref[...] = act_in[...]

    @pl.when(segment < turn)
    def _():
        write_message(act_in[...], coded[...], own, low, high)

    @pl.when(segment > turn)
    def _():
        write_message(x_in[...], coded[...], own, low, high)


def hot_kernel(row_map, x, hot):
    offsets, half = row_map.shape
    columns = row_map[...]
    within = jnp.where(columns >= 2 * half, -1, jnp.bitwise_and(columns, half - 1)).astype(F32)
    spare = jnp.zeros((-offsets % 8, half), F32)
    within = jnp.concatenate([within, spare], axis=0).T
    places = lax.broadcasted_iota(jnp.int32, (half, half), 1).astype(F32)
    for k in range(offsets):
        found = jnp.where(places == within[:, k : k + 1], jnp.ones((), F32), jnp.zeros((), F32))
        hot[k * half : (k + 1) * half, :] = found.astype(BF16)


def spread_body(dz, weight, row_map, masked, hot):
    offsets, channels = weight.shape[0], weight.shape[1]
    half = row_map.shape[1]
    for k in range(offsets):
        columns = row_map[k : k + 1, :]
        rows = jnp.dot(weight[k], dz, preferred_element_type=F32)
        upper = columns >= half
        zero = jnp.zeros((), F32)
        masked[:channels, k * half : (k + 1) * half] = jnp.where(upper, zero, rows).astype(BF16)
        masked[channels:, k * half : (k + 1) * half] = jnp.where(upper, rows, zero).astype(BF16)
    return jnp.dot(masked[...], hot[...], preferred_element_type=F32)


def face_terms(x, from_low, from_high):
    owner, count = lax.axis_index("space"), lax.axis_size("space")
    zero = jnp.zeros((), F32)
    lane = lax.broadcasted_iota(jnp.int32, (1, LANES), 1)
    has_low = lane + owner * LANES >= LANES
    has_high = lane + (owner + 1) * LANES < count * LANES
    low = jnp.where(has_low, from_low.astype(F32), zero)
    high = jnp.where(has_high, from_high.astype(F32), zero)
    return through_norm(x.astype(F32), jnp.concatenate([low, high], axis=1))


def slope_kernel(turn, segments, part_in, from_low, from_high, act, z, grad_in, dz_in, dz, grad):
    active = lax.axis_index("segment") == turn

    @pl.when(active)
    def _():
        if turn == segments - 1:
            total = grad_in[...]
        else:
            channels = act.shape[0]
            total = part_in[:channels, :].astype(F32) + face_terms(
                act[...], from_low[:channels, :], from_high[:channels, :]
            )
        grad[...] = total
        dz[...] = (total * silu_slope(z[...])).astype(BF16)

    @pl.when(jnp.logical_not(active))
    def _():
        dz[...] = dz_in[...]
        grad[...] = grad_in[...]


def spread_kernel(
    turn, dz, grad, x, act, weight, row_map, hot, coded, part_in, low_in, high_in, *refs
):
    (part, low, high), message, masked = refs[:3], refs[3:-1], refs[-1]
    active = lax.axis_index("segment") == turn

    @pl.when(active)
    def _():
        channels = x.shape[0]
        table = spread_body(dz[...], weight, row_map, masked, hot)
        own = jnp.concatenate([table[:channels, LANES:], table[channels:, :LANES]], axis=1)
        total = grad[...] + through_norm(x[...].astype(F32), own)
        part[...] = total
        to_low = table[:channels, :LANES].astype(BF16)
        to_high = table[channels:, LANES:].astype(BF16)
        low[...] = to_low
        high[...] = to_high
        if message:
            write_message(total.astype(BF16), coded[...], *message)
            message[1][:channels, :] = to_low
            message[2][:channels, :] = to_high

    @pl.when(jnp.logical_not(active))
    def _():
        part[...] = part_in[...]
        low[...] = low_in[...]
        high[...] = high_in[...]

    if message:
        segment = lax.axis_index("segment")

        @pl.when(segment == turn - 1)
        def _():
            write_message(act[...], coded[...], *message)

        @pl.when(jnp.logical_and(segment != turn, segment != turn - 1))
        def _():
            write_message(x[...], coded[...], *message)


def order_kernel(low, high, one, two):
    even = even_segment()
    one[...] = jnp.where(even, high[...], low[...])
    two[...] = jnp.where(even, low[...], high[...])


def finish_kernel(part, x, one, two, out):
    even = even_segment()
    from_low = jnp.where(even, one[...], two[...])
    from_high = jnp.where(even, two[...], one[...])
    out[...] = (part[...] + face_terms(x[...], from_low, from_high)).astype(BF16)


def decoded_columns(coded):
    coded = coded.astype(F32)
    return jnp.where(coded < 0.0, 256.0 - coded, coded).astype(jnp.int32)


def assemble_kernel(numbers, x, coded, *refs):
    received, out = refs[:-1], refs[-1]
    segment = lax.axis_index("segment")
    channels = x.shape[0]
    out[0, :channels, :] = x[...]
    out[0, channels:, :] = coded[...]
    for number in numbers:

        @pl.when(segment == number)
        def _(number=number):
            one, two, three = (received[3 * came : 3 * came + 3] for came in CAME[number])
            out[1] = one[0][...]
            out[2, :, :LANES] = two[1][...]
            out[2, :, LANES:] = two[2][...]
            out[3] = three[0][...]


def join_kernel(*refs):
    place = 0
    for ref in refs[:-1]:
        for i in range(ref.shape[0]):
            refs[-1][place] = ref[i]
            place += 1


def join(name, *stacks):
    shape = (sum(stack.shape[0] for stack in stacks),) + stacks[0].shape[1:]
    return call(join_kernel, name, struct(shape, stacks[0].dtype), *stacks)


def picked_body(channels, offsets, side, mine, other, picked, table):
    half, rows = mine.shape[0], mine.shape[2]
    owners = 2 * half
    me = lax.axis_index("space")
    for block in range(owners):
        source = mine if block < half else other
        table[block] = normalized(source[block % half][:channels])

    def place(owner):
        away = jnp.bitwise_xor(me, owner)
        return jnp.bitwise_and(away, 1) * half + jnp.right_shift(away, 1)

    for block in range(half):
        q = jnp.bitwise_xor(me, 2 * block + side)
        low = table[place(jnp.maximum(q - 1, 0))][:, LANES:]
        high = table[place(jnp.minimum(q + 1, owners - 1))][:, :LANES]
        lookup = stacked_lookup(low, table[side * half + block], high)
        columns = decoded_columns((other if side else mine)[block][channels:])

        def store(k, rows_of_k, block=block):
            span = slice(block * rows, (block + 1) * rows)
            picked[k * channels : (k + 1) * channels, span] = rows_of_k

        pick_all(lookup, columns[:offsets, :], store)


def picked_kernel(channels, offsets, side, first, mine, other, *refs):
    picked, table = refs[-2:]
    segment = lax.axis_index("segment")

    @pl.when(segment == 0 if first else segment != 0)
    def _():
        picked_body(channels, offsets, side, mine, other, picked, table)


def weight_kernel(factor, picked, slopes, *refs):
    out = refs[-1]
    slopes = jnp.concatenate([slopes[i] for i in range(slopes.shape[0])], axis=1)
    offsets, channels = out.shape[0], out.shape[1]
    for k in range(offsets):
        total = lax.dot_general(
            picked[k * channels : (k + 1) * channels, :],
            slopes,
            (((1,), (1,)), ((), ())),
            preferred_element_type=F32,
        )
        for ref in refs[:-1]:
            total = total + ref[k]
        out[k] = factor * total


def last_kernel(factor, picked, slopes, before, part, x, one, two, weight_grad, grad_in):
    finish_kernel(part, x, one, two, grad_in)
    weight_kernel(factor, picked, slopes, before, weight_grad)


def lone_picked_kernel(low, own, high, row_map, picked):
    channels = own.shape[0]
    lookup = stacked_lookup(normalized(low[...]), normalized(own[...]), normalized(high[...]))
    for k in range(row_map.shape[0]):
        picked[k * channels : (k + 1) * channels, :] = pick_rows(lookup, row_map[k : k + 1, :])


def per_device(features, weights, row_map, block_count, cotangent):
    channels, rows = features.shape
    segments, count = lax.axis_size("segment"), lax.axis_size("space")
    offsets = row_map.shape[0]
    weight = weights[0]
    wide, face = (channels, rows), (channels, LANES)
    flops = 2 * offsets * channels * channels * rows
    live = (jnp.arange(rows, dtype=jnp.int32) < block_count[0] * LANES).astype(F32)[None, :]
    everyone = count == 8 and segments == 4

    current, one, two = call(
        prepare_kernel,
        "prepare",
        [struct(wide, BF16), struct(face, BF16), struct(face, BF16)],
        features,
        live,
        far=1,
        scratch=[pltpu.VMEM(wide, BF16), pltpu.SemaphoreType.DMA],
    )
    first, second = halo_pairs(segments, count)
    low, high = lax.ppermute(one, AXES, first), lax.ppermute(two, AXES, second)
    padded = -(-offsets // 16) * 16
    weight, row_map, coded = call(
        load_kernel,
        "load",
        [
            struct(weight.shape, BF16),
            struct(row_map.shape, jnp.int32),
            struct((padded, rows), BF16),
        ],
        weight,
        row_map,
        current,
        far=2,
        scratch=[pltpu.SemaphoreType.DMA((2,))],
    )
    cores = [(p, p ^ 1) for p in range(count)]
    block, half_block = (channels + padded, rows), (channels + padded, LANES)
    message = [struct(block, BF16), struct(half_block, BF16), struct(half_block, BF16)]
    received = []

    def assemble(name, numbers, *others):
        used = 1 + max(max(CAME[number]) for number in numbers)
        arrays = sum(received[:used], ())
        return call(
            functools.partial(assemble_kernel, numbers),
            name,
            struct((count // 2,) + block, BF16),
            x,
            coded,
            *after_all(arrays, others),
        )

    def pick(side, first, mine, other, *before):
        return call(
            functools.partial(picked_kernel, channels, offsets, side, first),
            f"picked{side}{'early' if first else 'late'}",
            struct((offsets * channels, count // 2 * rows), BF16),
            mine,
            other,
            *before,
            limit=24 << 20,
            scratch=[pltpu.VMEM((count, channels, rows), BF16)],
            flops=4 * flops,
            aliases={2: 0} if before else {},
        )

    z = jnp.zeros(wide, F32)
    x = act = own = current
    picked = []
    for turn in range(segments):
        outputs = call(
            functools.partial(forward_kernel, turn),
            f"forward{turn}",
            message
            + [struct(wide, F32), struct(wide, BF16), struct(wide, BF16)]
            + [struct(wide, BF16)] * (turn + 1 == segments),
            own,
            low,
            high,
            weight,
            row_map,
            coded,
            live,
            z,
            x,
            act,
            scratch=[pltpu.VMEM((offsets * channels, rows), BF16)],
            flops=flops,
        )
        sent, (z, x, act) = outputs[:3], outputs[3:6]
        acts = outputs[-1]
        if turn == 0:
            grad = call(gradient_kernel, "gradient", struct(wide, F32), cotangent, live, x)
            hot = call(hot_kernel, "hot", struct((offsets * rows, rows), BF16), row_map, x)
        if turn + 1 < segments:
            if everyone and turn == segments - 2:
                early = assemble("early_rows", (0,), z)
                early_other = lax.ppermute(early, "space", cores)
            own, from_down, from_up = hop(
                len(received), turn, turn + 1, count, sent[1], sent[2], sent[0]
            )
            received.append((own, from_down, from_up))
            low, high = from_up, from_down

    dz = jnp.zeros(wide, BF16)
    part = grad
    out_low = out_high = jnp.zeros(face, BF16)
    for turn in reversed(range(segments)):
        own, from_high, from_low = received[-1]
        dz, grad = call(
            functools.partial(slope_kernel, turn, segments),
            f"slope{turn}",
            [struct(wide, BF16), struct(wide, F32)],
            own,
            from_low,
            from_high,
            act,
            z,
            grad,
            dz,
        )
        if turn == 0 and everyone:
            late = assemble("late_rows", tuple(range(1, segments)))
            slopes = [dz] + [
                lax.ppermute(dz, "space", [(p, p ^ (2 * m)) for p in range(count)])
                for m in range(1, count // 2)
            ]
            late_other = lax.ppermute(after(late, dz), "space", cores)
        part, out_low, out_high, *sent = call(
            functools.partial(spread_kernel, turn),
            f"spread{turn}",
            [struct(wide, F32), struct(face, BF16), struct(face, BF16)]
            + (message if turn > 0 else []),
            dz,
            grad,
            x,
            act,
            weight,
            row_map,
            hot,
            coded,
            part,
            out_low,
            out_high,
            scratch=[pltpu.VMEM((2 * channels, offsets * rows), BF16)],
            limit=16 << 20,
            flops=2 * flops,
        )
        if turn > 0:
            if everyone and len(picked) < 2:
                if not picked:
                    early_other = after(early_other, dz)
                picked.append(pick(len(picked), True, early, after(early_other, dz)))
                sent = after_all(sent, picked[-1:])
            received.append(
                hop(len(received), turn, turn - 1, count, sent[1], sent[2], sent[0])
            )

    one, two = call(
        order_kernel, "order", [struct(face, BF16), struct(face, BF16)], out_low, out_high
    )
    face_one, face_two = lax.ppermute(one, AXES, first), lax.ppermute(two, AXES, second)

    factor = 1.0 / math.sqrt(rows * count)
    shape = struct((offsets, channels, channels), F32)
    if everyone:
        picked = [pick(side, False, late, late_other, picked[side]) for side in range(2)]
        slopes = after_all(slopes, (one, two, picked[0]))
        slopes = join("slopes", *(block[None] for block in slopes))
        others = lax.ppermute(slopes, "space", cores)
        weight_grad = call(
            functools.partial(weight_kernel, 1.0),
            "weight_grad_mine",
            shape,
            picked[0],
            slopes,
            limit=24 << 20,
            flops=4 * flops,
        )
        face_one, face_two = after_all((face_one, face_two), (weight_grad, picked[1]))
        weight_grad, grad_in = call(
            functools.partial(last_kernel, factor),
            "last",
            [shape, struct(wide, BF16)],
            picked[1],
            others,
            weight_grad,
            part,
            x,
            face_one,
            face_two,
            limit=24 << 20,
            flops=4 * flops,
        )
    else:
        low = lax.ppermute(x[:, LANES:], "space", [(p, p + 1) for p in range(count - 1)])
        high = lax.ppermute(x[:, :LANES], "space", [(p, p - 1) for p in range(1, count)])
        picked = call(
            lone_picked_kernel,
            "lone_picked",
            struct((offsets * channels, rows), BF16),
            low,
            x,
            high,
            row_map,
        )
        weight_grad = call(
            functools.partial(weight_kernel, factor), "weight_grad", shape, picked, dz[None]
        )
        weight_grad = lax.psum(weight_grad, "space")
        grad_in = call(finish_kernel, "finish", struct(wide, BF16), part, x, face_one, face_two)
    return acts[None], grad_in[None], weight_grad[None]


def solution(mesh):
    placed = (
        P(None, "space"),
        P("segment", None, None, None),
        P(None, "space"),
        P("space"),
        P(None, "space"),
    )
    return jax.shard_map(
        per_device,
        mesh=mesh,
        in_specs=placed,
        out_specs=(
            P("segment", None, "space"),
            P("segment", None, "space"),
            P("segment", None, None, None),
        ),
        check_vma=False,
    )
```

```python
import functools
import math

import jax
import jax.numpy as jnp
from jax import lax
from jax.experimental import pallas as pl
from jax.experimental.pallas import tpu as pltpu
from jax.sharding import PartitionSpec as P

AXES = ("segment", "space")
BF16 = jnp.bfloat16
F32 = jnp.float32
LANES = 128
VMEM = pl.BlockSpec(memory_space=pltpu.VMEM)
HBM = pl.BlockSpec(memory_space=pltpu.HBM)


def call(body, name, out_shape, *args, limit=8 << 20, scratch=(), flops=0, far=0, aliases=None):
    return pl.pallas_call(
        body,
        name=name,
        out_shape=out_shape,
        in_specs=[HBM] * far + [VMEM] * (len(args) - far),
        out_specs=jax.tree.map(lambda _: VMEM, out_shape),
        scratch_shapes=list(scratch),
        input_output_aliases=aliases or {},
        compiler_params=pltpu.CompilerParams(vmem_limit_bytes=limit),
        cost_estimate=pl.CostEstimate(flops=flops, bytes_accessed=0, transcendentals=0),
    )(*args)


def after(value, *others):
    return lax.optimization_barrier((value,) + others)[0]


def after_all(values, others):
    return lax.optimization_barrier((*values, *others))[: len(values)]


def struct(shape, dtype):
    return jax.ShapeDtypeStruct(shape, dtype)


BESIDE_OWN = (
    (2, ((2, 2, 1), (3, 3, 1))),
    (0, ((3, 0, 6), (0, 3, 0))),
    (0, ((0, 1, 2), (1, 0, 0))),
    (2, ((1, 1, 6), (0, 0, 1))),
    (6, ((3, 3, 6), (0, 0, 1))),
    (0, ((2, 2, 2), (3, 3, 1))),
)
BESIDE_FACES = (
    (4, (3, 3), ((2, 2, 1),)),
    (0, (3, 3), ((0, 0, 1),)),
    (0, (1, 0), ((0, 1, 4),)),
    (4, (0, 0), ((1, 1, 1),)),
    (4, (3, 3), ((0, 0, 1),)),
    (0, (3, 3), ((2, 2, 1),)),
)
CAME = {0: (0, 0, 1), 1: (2, 2, 3), 2: (5, 4, 4), 3: (3, 3, 4)}


def hop_pairs(number, source, target, count):
    def at(segment, owner):
        return segment * count + owner

    def moves(sends):
        return [(at(a, p), at(b, p ^ step)) for a, b, step in sends for p in range(count)]

    last = count - 1
    back, rest = BESIDE_OWN[number]
    own = [(at(source, p), at(target, p)) for p in range(count)]
    own += moves(((target, source, back),) + rest)
    back, (leave, enter), rest = BESIDE_FACES[number]
    both = moves(((target, source, back),) + rest)
    down = both + [(at(source, p), at(target, p - 1)) for p in range(1, count)]
    down += [(at(leave, p), at(enter, p + 1)) for p in range(last)]
    down += [(at(source, 0), at(enter, 0)), (at(leave, last), at(target, last))]
    up = both + [(at(source, p), at(target, p + 1)) for p in range(last)]
    up += [(at(leave, p), at(enter, p - 1)) for p in range(1, count)]
    up += [(at(source, last), at(enter, last)), (at(leave, 0), at(target, 0))]
    return sorted(own), sorted(down), sorted(up)


def hop(number, source, target, count, low, high, own):
    straight, down, up = hop_pairs(number, source, target, count)
    return (
        lax.ppermute(own, AXES, straight),
        lax.ppermute(low, AXES, down),
        lax.ppermute(high, AXES, up),
    )


def halo_pairs(segments, count):
    last = count - 1
    one, two = [], []
    for even in range(0, segments, 2):
        a, b = even * count, (even + 1) * count
        one += [(a + p, a + p + 1) for p in range(last)] + [(a + last, b + last)]
        one += [(b + p, b + p - 1) for p in range(1, count)] + [(b, a)]
        two += [(a + p, a + p - 1) for p in range(1, count)] + [(a, b)]
        two += [(b + p, b + p + 1) for p in range(last)] + [(b + last, a + last)]
    return sorted(one), sorted(two)


def rms_scale(x32):
    return lax.rsqrt(jnp.mean(x32 * x32, axis=0, keepdims=True) + 1e-5)


def normalized(x):
    x32 = x.astype(F32)
    return (x32 * rms_scale(x32)).astype(BF16)


def stacked_lookup(low, own, high):
    first = jnp.concatenate([low, own[:, :LANES]], axis=1)
    second = jnp.concatenate([own[:, LANES:], high], axis=1)
    return jnp.concatenate([first, second], axis=0)


def one_hot(columns, missing):
    half = columns.shape[1]
    within = jnp.where(columns >= missing, -1, jnp.bitwise_and(columns, half - 1))
    places = lax.broadcasted_iota(jnp.int32, (half, half), 0).astype(F32).astype(BF16)
    within = within.astype(F32).astype(BF16)
    return jnp.where(places == within, jnp.ones((), BF16), jnp.zeros((), BF16))


def pick_rows(lookup, columns):
    channels, half = lookup.shape[0] // 2, lookup.shape[1]
    found = jnp.dot(lookup, one_hot(columns, 2 * half), preferred_element_type=F32)
    return jnp.where(columns >= half, found[channels:], found[:channels]).astype(BF16)


def gather_rows(blocks, columns):
    halves = []
    for first in range(0, columns.shape[1], LANES):
        wanted = columns[:, first : first + LANES]
        lane = jnp.broadcast_to(jnp.bitwise_and(wanted, LANES - 1), blocks[0].shape)
        found = jnp.zeros((), F32)
        for place in reversed(range(len(blocks))):
            there = jnp.take_along_axis(blocks[place], lane, axis=1, mode="promise_in_bounds")
            found = jnp.where(wanted < (place + 1) * LANES, there, found)
        halves.append(found)
    return jnp.concatenate(halves, axis=1).astype(BF16)


def pick_all(lookup, columns, store, share=0):
    channels, offsets = lookup.shape[0] // 2, columns.shape[0]
    wide = lookup.astype(F32)
    blocks = [
        wide[half : half + channels, lane : lane + LANES]
        for half in (0, channels)
        for lane in (0, LANES)
    ]
    for k in range(offsets):
        row = columns[k : k + 1, :]
        gathered = (k * share) // offsets != ((k + 1) * share) // offsets
        store(k, gather_rows(blocks, row) if gathered else pick_rows(lookup, row))


def silu_slope(z):
    sigmoid = jax.nn.sigmoid(z)
    return sigmoid * (1.0 + z * (1.0 - sigmoid))


def through_norm(x32, grad):
    inverse = rms_scale(x32)
    mean = jnp.mean(x32 * grad, axis=0, keepdims=True)
    return inverse * grad - x32 * (inverse * inverse * inverse) * mean


def even_segment():
    return jnp.where(lax.rem(lax.axis_index("segment"), 2) == 0, 1.0, 0.0).astype(F32) > 0.5


def prepare_kernel(features, live, x, one, two, landing, sem):
    copy = pltpu.make_async_copy(features, landing, sem)
    copy.start()
    copy.wait()
    rows = jnp.where(live[...] > 0.0, landing[...].astype(F32), jnp.zeros((), F32)).astype(BF16)
    x[...] = rows
    low, high = rows[:, :LANES], rows[:, LANES:]
    up = even_segment()
    one[...] = jnp.where(up, high, low)
    two[...] = jnp.where(up, low, high)


def load_kernel(weight_in, map_in, x, weight, row_map, coded, sems):
    copies = [
        pltpu.make_async_copy(weight_in, weight, sems.at[0]),
        pltpu.make_async_copy(map_in, row_map, sems.at[1]),
    ]
    for copy in copies:
        copy.start()
    for copy in copies:
        copy.wait()
    columns = row_map[...]
    small = jnp.where(columns > 256, 256 - columns, columns).astype(F32)
    spare = jnp.zeros((coded.shape[0] - columns.shape[0], columns.shape[1]), F32)
    coded[...] = jnp.concatenate([small, spare], axis=0).astype(BF16)


def gradient_kernel(cotangent, live, x, grad):
    grad[...] = jnp.where(live[...] > 0.0, cotangent[...].astype(F32), jnp.zeros((), F32))


def write_message(rows, below, own, low, high):
    own[: rows.shape[0], :] = rows
    low[: rows.shape[0], :] = rows[:, :LANES]
    high[: rows.shape[0], :] = rows[:, LANES:]
    own[rows.shape[0] :, :] = below
    low[rows.shape[0] :, :] = below[:, :LANES]
    high[rows.shape[0] :, :] = below[:, LANES:]


def forward_kernel(turn, *refs):
    (own_in, low_in, high_in, weight, row_map, coded, live, z_in, x_in, act_in) = refs[:10]
    (own, low, high, z, x, act) = refs[10:16]
    picked, results = refs[-1], refs[16:-1]
    segment = lax.axis_index("segment")
    offsets, channels = weight.shape[0], weight.shape[1]

    @pl.when(segment == turn)
    def _():
        rows = own_in[:channels, :]
        lookup = stacked_lookup(
            normalized(low_in[:channels, :]), normalized(rows), normalized(high_in[:channels, :])
        )

        def store(k, rows_of_k):
            picked[k * channels : (k + 1) * channels, :] = rows_of_k

        pick_all(lookup, row_map[...], store, share=8)
        total = lax.dot_general(
            weight[...].reshape(offsets * channels, channels),
            picked[...],
            (((0,), (0,)), ((), ())),
            preferred_element_type=F32,
        )
        total = jnp.where(live[...] > 0.0, total, jnp.zeros((), F32))
        z[...] = total
        result = (rows.astype(F32) + total * jax.nn.sigmoid(total)).astype(BF16)
        write_message(result, coded[...], own, low, high)
        x[...] = rows
        act[...] = result
        for ref in results:
            ref[...] = result

    @pl.when(segment != turn)
    def _():
        z[...] = z_in[...]
        x[...] = x_in[...]
        act[...] = act_in[...]
        for ref in results:
            ref[...] = act_in[...]

    @pl.when(segment < turn)
    def _():
        write_message(act_in[...], coded[...], own, low, high)

    @pl.when(segment > turn)
    def _():
        write_message(x_in[...], coded[...], own, low, high)


def hot_kernel(row_map, x, hot):
    offsets, half = row_map.shape
    columns = row_map[...]
    within = jnp.where(columns >= 2 * half, -1, jnp.bitwise_and(columns, half - 1)).astype(F32)
    spare = jnp.zeros((-offsets % 8, half), F32)
    within = jnp.concatenate([within, spare], axis=0).T
    places = lax.broadcasted_iota(jnp.int32, (half, half), 1).astype(F32)
    for k in range(offsets):
        found = jnp.where(places == within[:, k : k + 1], jnp.ones((), F32), jnp.zeros((), F32))
        hot[k * half : (k + 1) * half, :] = found.astype(BF16)


def spread_body(dz, weight, row_map, masked, hot):
    offsets, channels = weight.shape[0], weight.shape[1]
    half = row_map.shape[1]
    for k in range(offsets):
        columns = row_map[k : k + 1, :]
        rows = jnp.dot(weight[k], dz, preferred_element_type=F32)
        upper = columns >= half
        zero = jnp.zeros((), F32)
        masked[:channels, k * half : (k + 1) * half] = jnp.where(upper, zero, rows).astype(BF16)
        masked[channels:, k * half : (k + 1) * half] = jnp.where(upper, rows, zero).astype(BF16)
    return jnp.dot(masked[...], hot[...], preferred_element_type=F32)


def face_terms(x, from_low, from_high):
    owner, count = lax.axis_index("space"), lax.axis_size("space")
    zero = jnp.zeros((), F32)
    lane = lax.broadcasted_iota(jnp.int32, (1, LANES), 1)
    has_low = lane + owner * LANES >= LANES
    has_high = lane + (owner + 1) * LANES < count * LANES
    low = jnp.where(has_low, from_low.astype(F32), zero)
    high = jnp.where(has_high, from_high.astype(F32), zero)
    return through_norm(x.astype(F32), jnp.concatenate([low, high], axis=1))


def slope_kernel(turn, segments, part_in, from_low, from_high, act, z, grad_in, dz_in, dz, grad):
    active = lax.axis_index("segment") == turn

    @pl.when(active)
    def _():
        if turn == segments - 1:
            total = grad_in[...]
        else:
            channels = act.shape[0]
            total = part_in[:channels, :].astype(F32) + face_terms(
                act[...], from_low[:channels, :], from_high[:channels, :]
            )
        grad[...] = total
        dz[...] = (total * silu_slope(z[...])).astype(BF16)

    @pl.when(jnp.logical_not(active))
    def _():
        dz[...] = dz_in[...]
        grad[...] = grad_in[...]


def spread_kernel(
    turn, dz, grad, x, act, weight, row_map, hot, coded, part_in, low_in, high_in, *refs
):
    (part, low, high), message, masked = refs[:3], refs[3:-1], refs[-1]
    active = lax.axis_index("segment") == turn

    @pl.when(active)
    def _():
        channels = x.shape[0]
        table = spread_body(dz[...], weight, row_map, masked, hot)
        own = jnp.concatenate([table[:channels, LANES:], table[channels:, :LANES]], axis=1)
        total = grad[...] + through_norm(x[...].astype(F32), own)
        part[...] = total
        to_low = table[:channels, :LANES].astype(BF16)
        to_high = table[channels:, LANES:].astype(BF16)
        low[...] = to_low
        high[...] = to_high
        if message:
            write_message(total.astype(BF16), coded[...], *message)
            message[1][:channels, :] = to_low
            message[2][:channels, :] = to_high

    @pl.when(jnp.logical_not(active))
    def _():
        part[...] = part_in[...]
        low[...] = low_in[...]
        high[...] = high_in[...]

    if message:
        segment = lax.axis_index("segment")

        @pl.when(segment == turn - 1)
        def _():
            write_message(act[...], coded[...], *message)

        @pl.when(jnp.logical_and(segment != turn, segment != turn - 1))
        def _():
            write_message(x[...], coded[...], *message)


def order_kernel(low, high, one, two):
    even = even_segment()
    one[...] = jnp.where(even, high[...], low[...])
    two[...] = jnp.where(even, low[...], high[...])


def finish_kernel(part, x, one, two, out):
    even = even_segment()
    from_low = jnp.where(even, one[...], two[...])
    from_high = jnp.where(even, two[...], one[...])
    out[...] = (part[...] + face_terms(x[...], from_low, from_high)).astype(BF16)


def decoded_columns(coded):
    coded = coded.astype(F32)
    return jnp.where(coded < 0.0, 256.0 - coded, coded).astype(jnp.int32)


def assemble_kernel(numbers, x, coded, *refs):
    received, out = refs[:-1], refs[-1]
    segment = lax.axis_index("segment")
    channels = x.shape[0]
    out[0, :channels, :] = x[...]
    out[0, channels:, :] = coded[...]
    for number in numbers:

        @pl.when(segment == number)
        def _(number=number):
            one, two, three = (received[3 * came : 3 * came + 3] for came in CAME[number])
            out[1] = one[0][...]
            out[2, :, :LANES] = two[1][...]
            out[2, :, LANES:] = two[2][...]
            out[3] = three[0][...]


def join_kernel(*refs):
    place = 0
    for ref in refs[:-1]:
        for i in range(ref.shape[0]):
            refs[-1][place] = ref[i]
            place += 1


def join(name, *stacks):
    shape = (sum(stack.shape[0] for stack in stacks),) + stacks[0].shape[1:]
    return call(join_kernel, name, struct(shape, stacks[0].dtype), *stacks)


def picked_body(channels, offsets, side, mine, other, picked, table):
    half, rows = mine.shape[0], mine.shape[2]
    owners = 2 * half
    me = lax.axis_index("space")
    for block in range(owners):
        source = mine if block < half else other
        table[block] = normalized(source[block % half][:channels])

    def place(owner):
        away = jnp.bitwise_xor(me, owner)
        return jnp.bitwise_and(away, 1) * half + jnp.right_shift(away, 1)

    for block in range(half):
        q = jnp.bitwise_xor(me, 2 * block + side)
        low = table[place(jnp.maximum(q - 1, 0))][:, LANES:]
        high = table[place(jnp.minimum(q + 1, owners - 1))][:, :LANES]
        lookup = stacked_lookup(low, table[side * half + block], high)
        columns = decoded_columns((other if side else mine)[block][channels:])

        def store(k, rows_of_k, block=block):
            span = slice(block * rows, (block + 1) * rows)
            picked[k * channels : (k + 1) * channels, span] = rows_of_k

        pick_all(lookup, columns[:offsets, :], store)


def picked_kernel(channels, offsets, side, first, mine, other, *refs):
    picked, table = refs[-2:]
    segment = lax.axis_index("segment")

    @pl.when(segment == 0 if first else segment != 0)
    def _():
        picked_body(channels, offsets, side, mine, other, picked, table)


def weight_kernel(factor, picked, slopes, *refs):
    out = refs[-1]
    slopes = jnp.concatenate([slopes[i] for i in range(slopes.shape[0])], axis=1)
    offsets, channels = out.shape[0], out.shape[1]
    for k in range(offsets):
        total = lax.dot_general(
            picked[k * channels : (k + 1) * channels, :],
            slopes,
            (((1,), (1,)), ((), ())),
            preferred_element_type=F32,
        )
        for ref in refs[:-1]:
            total = total + ref[k]
        out[k] = factor * total


def last_kernel(factor, picked, slopes, before, part, x, one, two, weight_grad, grad_in):
    finish_kernel(part, x, one, two, grad_in)
    weight_kernel(factor, picked, slopes, before, weight_grad)


def lone_picked_kernel(low, own, high, row_map, picked):
    channels = own.shape[0]
    lookup = stacked_lookup(normalized(low[...]), normalized(own[...]), normalized(high[...]))
    for k in range(row_map.shape[0]):
        picked[k * channels : (k + 1) * channels, :] = pick_rows(lookup, row_map[k : k + 1, :])


def per_device(features, weights, row_map, block_count, cotangent):
    channels, rows = features.shape
    segments, count = lax.axis_size("segment"), lax.axis_size("space")
    offsets = row_map.shape[0]
    weight = weights[0]
    wide, face = (channels, rows), (channels, LANES)
    flops = 2 * offsets * channels * channels * rows
    live = (jnp.arange(rows, dtype=jnp.int32) < block_count[0] * LANES).astype(F32)[None, :]
    everyone = count == 8 and segments == 4

    current, one, two = call(
        prepare_kernel,
        "prepare",
        [struct(wide, BF16), struct(face, BF16), struct(face, BF16)],
        features,
        live,
        far=1,
        scratch=[pltpu.VMEM(wide, BF16), pltpu.SemaphoreType.DMA],
    )
    first, second = halo_pairs(segments, count)
    low, high = lax.ppermute(one, AXES, first), lax.ppermute(two, AXES, second)
    padded = -(-offsets // 16) * 16
    weight, row_map, coded = call(
        load_kernel,
        "load",
        [
            struct(weight.shape, BF16),
            struct(row_map.shape, jnp.int32),
            struct((padded, rows), BF16),
        ],
        weight,
        row_map,
        current,
        far=2,
        scratch=[pltpu.SemaphoreType.DMA((2,))],
    )
    cores = [(p, p ^ 1) for p in range(count)]
    block, half_block = (channels + padded, rows), (channels + padded, LANES)
    message = [struct(block, BF16), struct(half_block, BF16), struct(half_block, BF16)]
    received = []

    def assemble(name, numbers, *others):
        used = 1 + max(max(CAME[number]) for number in numbers)
        arrays = sum(received[:used], ())
        return call(
            functools.partial(assemble_kernel, numbers),
            name,
            struct((count // 2,) + block, BF16),
            x,
            coded,
            *after_all(arrays, others),
        )

    def pick(side, first, mine, other, *before):
        return call(
            functools.partial(picked_kernel, channels, offsets, side, first),
            f"picked{side}{'early' if first else 'late'}",
            struct((offsets * channels, count // 2 * rows), BF16),
            mine,
            other,
            *before,
            limit=24 << 20,
            scratch=[pltpu.VMEM((count, channels, rows), BF16)],
            flops=4 * flops,
            aliases={2: 0} if before else {},
        )

    z = jnp.zeros(wide, F32)
    x = act = own = current
    picked = []
    for turn in range(segments):
        outputs = call(
            functools.partial(forward_kernel, turn),
            f"forward{turn}",
            message
            + [struct(wide, F32), struct(wide, BF16), struct(wide, BF16)]
            + [struct(wide, BF16)] * (turn + 1 == segments),
            own,
            low,
            high,
            weight,
            row_map,
            coded,
            live,
            z,
            x,
            act,
            scratch=[pltpu.VMEM((offsets * channels, rows), BF16)],
            flops=flops,
        )
        sent, (z, x, act) = outputs[:3], outputs[3:6]
        acts = outputs[-1]
        if turn == 0:
            grad = call(gradient_kernel, "gradient", struct(wide, F32), cotangent, live, x)
            hot = call(hot_kernel, "hot", struct((offsets * rows, rows), BF16), row_map, x)
        if turn + 1 < segments:
            if everyone and turn == segments - 2:
                early = assemble("early_rows", (0,), z)
                early_other = lax.ppermute(early, "space", cores)
            own, from_down, from_up = hop(
                len(received), turn, turn + 1, count, sent[1], sent[2], sent[0]
            )
            received.append((own, from_down, from_up))
            low, high = from_up, from_down

    dz = jnp.zeros(wide, BF16)
    part = grad
    out_low = out_high = jnp.zeros(face, BF16)
    for turn in reversed(range(segments)):
        own, from_high, from_low = received[-1]
        dz, grad = call(
            functools.partial(slope_kernel, turn, segments),
            f"slope{turn}",
            [struct(wide, BF16), struct(wide, F32)],
            own,
            from_low,
            from_high,
            act,
            z,
            grad,
            dz,
        )
        if turn == 0 and everyone:
            late = assemble("late_rows", tuple(range(1, segments)))
            slopes = [dz] + [
                lax.ppermute(dz, "space", [(p, p ^ (2 * m)) for p in range(count)])
                for m in range(1, count // 2)
            ]
            late_other = lax.ppermute(after(late, dz), "space", cores)
        part, out_low, out_high, *sent = call(
            functools.partial(spread_kernel, turn),
            f"spread{turn}",
            [struct(wide, F32), struct(face, BF16), struct(face, BF16)]
            + (message if turn > 0 else []),
            dz,
            grad,
            x,
            act,
            weight,
            row_map,
            hot,
            coded,
            part,
            out_low,
            out_high,
            scratch=[pltpu.VMEM((2 * channels, offsets * rows), BF16)],
            limit=16 << 20,
            flops=2 * flops,
        )
        if turn > 0:
            if everyone and len(picked) < 2:
                if not picked:
                    early_other = after(early_other, dz)
                picked.append(pick(len(picked), True, early, after(early_other, dz)))
                sent = after_all(sent, picked[-1:])
            received.append(
                hop(len(received), turn, turn - 1, count, sent[1], sent[2], sent[0])
            )

    one, two = call(
        order_kernel, "order", [struct(face, BF16), struct(face, BF16)], out_low, out_high
    )
    face_one, face_two = lax.ppermute(one, AXES, first), lax.ppermute(two, AXES, second)

    factor = 1.0 / math.sqrt(rows * count)
    shape = struct((offsets, channels, channels), F32)
    if everyone:
        picked = [pick(side, False, late, late_other, picked[side]) for side in range(2)]
        slopes = after_all(slopes, (one, two, picked[0]))
        slopes = join("slopes", *(block[None] for block in slopes))
        others = lax.ppermute(slopes, "space", cores)
        weight_grad = call(
            functools.partial(weight_kernel, 1.0),
            "weight_grad_mine",
            shape,
            picked[0],
            slopes,
            limit=24 << 20,
            flops=4 * flops,
        )
        face_one, face_two = after_all((face_one, face_two), (weight_grad, picked[1]))
        weight_grad, grad_in = call(
            functools.partial(last_kernel, factor),
            "last",
            [shape, struct(wide, BF16)],
            picked[1],
            others,
            weight_grad,
            part,
            x,
            face_one,
            face_two,
            limit=24 << 20,
            flops=4 * flops,
        )
    else:
        low = lax.ppermute(x[:, LANES:], "space", [(p, p + 1) for p in range(count - 1)])
        high = lax.ppermute(x[:, :LANES], "space", [(p, p - 1) for p in range(1, count)])
        picked = call(
            lone_picked_kernel,
            "lone_picked",
            struct((offsets * channels, rows), BF16),
            low,
            x,
            high,
            row_map,
        )
        weight_grad = call(
            functools.partial(weight_kernel, factor), "weight_grad", shape, picked, dz[None]
        )
        weight_grad = lax.psum(weight_grad, "space")
        grad_in = call(finish_kernel, "finish", struct(wide, BF16), part, x, face_one, face_two)
    return acts[None], grad_in[None], weight_grad[None]


def solution(mesh):
    placed = (
        P(None, "space"),
        P("segment", None, None, None),
        P(None, "space"),
        P("space"),
        P(None, "space"),
    )
    return jax.shard_map(
        per_device,
        mesh=mesh,
        in_specs=placed,
        out_specs=(
            P("segment", None, "space"),
            P("segment", None, "space"),
            P("segment", None, None, None),
        ),
        check_vma=False,
    )
```

```python
import functools
import math

import jax
import jax.numpy as jnp
from jax import lax
from jax.experimental import pallas as pl
from jax.experimental.pallas import tpu as pltpu
from jax.sharding import PartitionSpec as P

AXES = ("segment", "space")
BF16 = jnp.bfloat16
F32 = jnp.float32
LANES = 128
VMEM = pl.BlockSpec(memory_space=pltpu.VMEM)
HBM = pl.BlockSpec(memory_space=pltpu.HBM)


def call(body, name, out_shape, *args, limit=8 << 20, scratch=(), flops=0, far=0, aliases=None):
    return pl.pallas_call(
        body,
        name=name,
        out_shape=out_shape,
        in_specs=[HBM] * far + [VMEM] * (len(args) - far),
        out_specs=jax.tree.map(lambda _: VMEM, out_shape),
        scratch_shapes=list(scratch),
        input_output_aliases=aliases or {},
        compiler_params=pltpu.CompilerParams(vmem_limit_bytes=limit),
        cost_estimate=pl.CostEstimate(flops=flops, bytes_accessed=0, transcendentals=0),
    )(*args)


def after(value, *others):
    return lax.optimization_barrier((value,) + others)[0]


def after_all(values, others):
    return lax.optimization_barrier((*values, *others))[: len(values)]


def struct(shape, dtype):
    return jax.ShapeDtypeStruct(shape, dtype)


BESIDE_OWN = (
    (4, ((2, 2, 1), (3, 3, 1))),
    (0, ((3, 0, 6), (0, 3, 0))),
    (0, ((0, 1, 2), (1, 0, 0))),
    (4, ((1, 1, 6), (0, 0, 1))),
    (6, ((3, 3, 6), (0, 0, 1))),
    (0, ((2, 2, 2), (3, 3, 1))),
)
BESIDE_FACES = (
    (2, (3, 3), ((2, 2, 1),)),
    (0, (3, 3), ((0, 0, 1),)),
    (0, (1, 0), ((0, 1, 4),)),
    (2, (0, 0), ((1, 1, 1),)),
    (4, (3, 3), ((0, 0, 1),)),
    (0, (3, 3), ((2, 2, 1),)),
)
CAME = {
    0: ((0, False), (0, True), (1, True)),
    1: ((2, True), (2, False), (3, True)),
    2: ((5, True), (4, False), (4, True)),
    3: ((3, False), (3, True), (4, True)),
}


def hop_pairs(number, source, target, count):
    def at(segment, owner):
        return segment * count + owner

    def moves(sends):
        return [(at(a, p), at(b, p ^ step)) for a, b, step in sends for p in range(count)]

    last = count - 1
    back, rest = BESIDE_OWN[number]
    own = [(at(source, p), at(target, p)) for p in range(count)]
    own += moves(((target, source, back),) + rest)
    back, (leave, enter), rest = BESIDE_FACES[number]
    both = moves(((target, source, back),) + rest)
    down = both + [(at(source, p), at(target, p - 1)) for p in range(1, count)]
    down += [(at(leave, p), at(enter, p + 1)) for p in range(last)]
    down += [(at(source, 0), at(enter, 0)), (at(leave, last), at(target, last))]
    up = both + [(at(source, p), at(target, p + 1)) for p in range(last)]
    up += [(at(leave, p), at(enter, p - 1)) for p in range(1, count)]
    up += [(at(source, last), at(enter, last)), (at(leave, 0), at(target, 0))]
    return sorted(own), sorted(down), sorted(up)


def hop(number, source, target, count, low, high, own):
    straight, down, up = hop_pairs(number, source, target, count)
    return (
        lax.ppermute(own, AXES, straight),
        lax.ppermute(low, AXES, down),
        lax.ppermute(high, AXES, up),
    )


def halo_pairs(segments, count):
    last = count - 1
    one, two = [], []
    for even in range(0, segments, 2):
        a, b = even * count, (even + 1) * count
        one += [(a + p, a + p + 1) for p in range(last)] + [(a + last, b + last)]
        one += [(b + p, b + p - 1) for p in range(1, count)] + [(b, a)]
        two += [(a + p, a + p - 1) for p in range(1, count)] + [(a, b)]
        two += [(b + p, b + p + 1) for p in range(last)] + [(b + last, a + last)]
    return sorted(one), sorted(two)


def rms_scale(x32):
    return lax.rsqrt(jnp.mean(x32 * x32, axis=0, keepdims=True) + 1e-5)


def normalized(x):
    x32 = x.astype(F32)
    return (x32 * rms_scale(x32)).astype(BF16)


def stacked_lookup(low, own, high):
    first = jnp.concatenate([low, own[:, :LANES]], axis=1)
    second = jnp.concatenate([own[:, LANES:], high], axis=1)
    return jnp.concatenate([first, second], axis=0)


def one_hot(columns, missing):
    half = columns.shape[1]
    within = jnp.where(columns >= missing, -1, jnp.bitwise_and(columns, half - 1))
    places = lax.broadcasted_iota(jnp.int32, (half, half), 0).astype(F32).astype(BF16)
    within = within.astype(F32).astype(BF16)
    return jnp.where(places == within, jnp.ones((), BF16), jnp.zeros((), BF16))


def pick_rows(lookup, columns):
    channels, half = lookup.shape[0] // 2, lookup.shape[1]
    found = jnp.dot(lookup, one_hot(columns, 2 * half), preferred_element_type=F32)
    return jnp.where(columns >= half, found[channels:], found[:channels]).astype(BF16)


def gather_rows(blocks, columns):
    halves = []
    for first in range(0, columns.shape[1], LANES):
        wanted = columns[:, first : first + LANES]
        lane = jnp.broadcast_to(jnp.bitwise_and(wanted, LANES - 1), blocks[0].shape)
        found = jnp.zeros((), F32)
        for place in reversed(range(len(blocks))):
            there = jnp.take_along_axis(blocks[place], lane, axis=1, mode="promise_in_bounds")
            found = jnp.where(wanted < (place + 1) * LANES, there, found)
        halves.append(found)
    return jnp.concatenate(halves, axis=1).astype(BF16)


def pick_all(lookup, columns, store, share=0):
    channels, offsets = lookup.shape[0] // 2, columns.shape[0]
    wide = lookup.astype(F32)
    blocks = [
        wide[half : half + channels, lane : lane + LANES]
        for half in (0, channels)
        for lane in (0, LANES)
    ]
    for k in range(offsets):
        row = columns[k : k + 1, :]
        gathered = (k * share) // offsets != ((k + 1) * share) // offsets
        store(k, gather_rows(blocks, row) if gathered else pick_rows(lookup, row))


def silu_slope(z):
    sigmoid = jax.nn.sigmoid(z)
    return sigmoid * (1.0 + z * (1.0 - sigmoid))


def through_norm(x32, grad):
    inverse = rms_scale(x32)
    mean = jnp.mean(x32 * grad, axis=0, keepdims=True)
    return inverse * grad - x32 * (inverse * inverse * inverse) * mean


def even_segment():
    return jnp.where(lax.rem(lax.axis_index("segment"), 2) == 0, 1.0, 0.0).astype(F32) > 0.5


def prepare_kernel(features, live, x, one, two, landing, sem):
    copy = pltpu.make_async_copy(features, landing, sem)
    copy.start()
    copy.wait()
    rows = jnp.where(live[...] > 0.0, landing[...].astype(F32), jnp.zeros((), F32)).astype(BF16)
    x[...] = rows
    low, high = rows[:, :LANES], rows[:, LANES:]
    up = even_segment()
    one[...] = jnp.where(up, high, low)
    two[...] = jnp.where(up, low, high)


def load_kernel(weight_in, map_in, x, weight, row_map, coded, sems):
    copies = [
        pltpu.make_async_copy(weight_in, weight, sems.at[0]),
        pltpu.make_async_copy(map_in, row_map, sems.at[1]),
    ]
    for copy in copies:
        copy.start()
    for copy in copies:
        copy.wait()
    columns = row_map[...]
    small = jnp.where(columns > 256, 256 - columns, columns).astype(F32)
    spare = jnp.zeros((coded.shape[0] - columns.shape[0], columns.shape[1]), F32)
    coded[...] = jnp.concatenate([small, spare], axis=0).astype(BF16)


def gradient_kernel(cotangent, live, x, grad):
    grad[...] = jnp.where(live[...] > 0.0, cotangent[...].astype(F32), jnp.zeros((), F32))


def write_message(rows, below, own, low, high):
    own[: rows.shape[0], :] = rows
    low[: rows.shape[0], :] = rows[:, :LANES]
    high[: rows.shape[0], :] = rows[:, LANES:]
    own[rows.shape[0] :, :] = below
    low[rows.shape[0] :, :] = below[:, :LANES]
    high[rows.shape[0] :, :] = below[:, LANES:]


def forward_kernel(turn, *refs):
    (own_in, low_in, high_in, weight, row_map, coded, live, z_in, x_in, act_in) = refs[:10]
    (own, low, high, z, x, act) = refs[10:16]
    picked, results = refs[-1], refs[16:-1]
    segment = lax.axis_index("segment")
    offsets, channels = weight.shape[0], weight.shape[1]

    @pl.when(segment == turn)
    def _():
        rows = own_in[:channels, :]
        lookup = stacked_lookup(
            normalized(low_in[:channels, :]), normalized(rows), normalized(high_in[:channels, :])
        )

        def store(k, rows_of_k):
            picked[k * channels : (k + 1) * channels, :] = rows_of_k

        pick_all(lookup, row_map[...], store, share=8)
        total = lax.dot_general(
            weight[...].reshape(offsets * channels, channels),
            picked[...],
            (((0,), (0,)), ((), ())),
            preferred_element_type=F32,
        )
        total = jnp.where(live[...] > 0.0, total, jnp.zeros((), F32))
        z[...] = total
        result = (rows.astype(F32) + total * jax.nn.sigmoid(total)).astype(BF16)
        write_message(result, coded[...], own, low, high)
        x[...] = rows
        act[...] = result
        for ref in results:
            ref[...] = result

    @pl.when(segment != turn)
    def _():
        z[...] = z_in[...]
        x[...] = x_in[...]
        act[...] = act_in[...]
        for ref in results:
            ref[...] = act_in[...]

    @pl.when(segment < turn)
    def _():
        write_message(act_in[...], coded[...], own, low, high)

    @pl.when(segment > turn)
    def _():
        write_message(x_in[...], coded[...], own, low, high)


def hot_kernel(row_map, x, hot):
    offsets, half = row_map.shape
    columns = row_map[...]
    within = jnp.where(columns >= 2 * half, -1, jnp.bitwise_and(columns, half - 1)).astype(F32)
    spare = jnp.zeros((-offsets % 8, half), F32)
    within = jnp.concatenate([within, spare], axis=0).T
    places = lax.broadcasted_iota(jnp.int32, (half, half), 1).astype(F32)
    for k in range(offsets):
        found = jnp.where(places == within[:, k : k + 1], jnp.ones((), F32), jnp.zeros((), F32))
        hot[k * half : (k + 1) * half, :] = found.astype(BF16)


def spread_body(dz, weight, row_map, masked, hot):
    offsets, channels = weight.shape[0], weight.shape[1]
    half = row_map.shape[1]
    for k in range(offsets):
        columns = row_map[k : k + 1, :]
        rows = jnp.dot(weight[k], dz, preferred_element_type=F32)
        upper = columns >= half
        zero = jnp.zeros((), F32)
        masked[:channels, k * half : (k + 1) * half] = jnp.where(upper, zero, rows).astype(BF16)
        masked[channels:, k * half : (k + 1) * half] = jnp.where(upper, rows, zero).astype(BF16)
    return jnp.dot(masked[...], hot[...], preferred_element_type=F32)


def face_terms(x, from_low, from_high):
    owner, count = lax.axis_index("space"), lax.axis_size("space")
    zero = jnp.zeros((), F32)
    lane = lax.broadcasted_iota(jnp.int32, (1, LANES), 1)
    has_low = lane + owner * LANES >= LANES
    has_high = lane + (owner + 1) * LANES < count * LANES
    low = jnp.where(has_low, from_low.astype(F32), zero)
    high = jnp.where(has_high, from_high.astype(F32), zero)
    return through_norm(x.astype(F32), jnp.concatenate([low, high], axis=1))


def slope_kernel(turn, segments, part_in, from_low, from_high, act, z, grad_in, dz_in, dz, grad):
    active = lax.axis_index("segment") == turn

    @pl.when(active)
    def _():
        if turn == segments - 1:
            total = grad_in[...]
        else:
            channels = act.shape[0]
            total = part_in[:channels, :].astype(F32) + face_terms(
                act[...], from_low[:channels, :], from_high[:channels, :]
            )
        grad[...] = total
        dz[...] = (total * silu_slope(z[...])).astype(BF16)

    @pl.when(jnp.logical_not(active))
    def _():
        dz[...] = dz_in[...]
        grad[...] = grad_in[...]


def spread_kernel(
    turn, dz, grad, x, act, weight, row_map, hot, coded, part_in, low_in, high_in, *refs
):
    (part, low, high), message, masked = refs[:3], refs[3:-1], refs[-1]
    active = lax.axis_index("segment") == turn

    @pl.when(active)
    def _():
        channels = x.shape[0]
        table = spread_body(dz[...], weight, row_map, masked, hot)
        own = jnp.concatenate([table[:channels, LANES:], table[channels:, :LANES]], axis=1)
        total = grad[...] + through_norm(x[...].astype(F32), own)
        part[...] = total
        to_low = table[:channels, :LANES].astype(BF16)
        to_high = table[channels:, LANES:].astype(BF16)
        low[...] = to_low
        high[...] = to_high
        if message:
            write_message(total.astype(BF16), coded[...], *message)
            message[1][:channels, :] = to_low
            message[2][:channels, :] = to_high

    @pl.when(jnp.logical_not(active))
    def _():
        part[...] = part_in[...]
        low[...] = low_in[...]
        high[...] = high_in[...]

    if message:
        segment = lax.axis_index("segment")

        @pl.when(segment == turn - 1)
        def _():
            write_message(act[...], coded[...], *message)

        @pl.when(jnp.logical_and(segment != turn, segment != turn - 1))
        def _():
            write_message(x[...], coded[...], *message)


def order_kernel(low, high, one, two):
    even = even_segment()
    one[...] = jnp.where(even, high[...], low[...])
    two[...] = jnp.where(even, low[...], high[...])


def finish_kernel(part, x, one, two, out):
    even = even_segment()
    from_low = jnp.where(even, one[...], two[...])
    from_high = jnp.where(even, two[...], one[...])
    out[...] = (part[...] + face_terms(x[...], from_low, from_high)).astype(BF16)


def decoded_columns(coded):
    coded = coded.astype(F32)
    return jnp.where(coded < 0.0, 256.0 - coded, coded).astype(jnp.int32)


def assemble_kernel(numbers, x, coded, *refs):
    received, out = refs[:-1], refs[-1]
    segment = lax.axis_index("segment")
    channels = x.shape[0]
    out[0, :channels, :] = x[...]
    out[0, channels:, :] = coded[...]
    for number in numbers:

        @pl.when(segment == number)
        def _(number=number):
            for place, (came, whole) in enumerate(CAME[number]):
                if whole:
                    out[place + 1] = received[3 * came][...]
                else:
                    out[place + 1, :, :LANES] = received[3 * came + 1][...]
                    out[place + 1, :, LANES:] = received[3 * came + 2][...]


def join_kernel(*refs):
    place = 0
    for ref in refs[:-1]:
        for i in range(ref.shape[0]):
            refs[-1][place] = ref[i]
            place += 1


def join(name, *stacks):
    shape = (sum(stack.shape[0] for stack in stacks),) + stacks[0].shape[1:]
    return call(join_kernel, name, struct(shape, stacks[0].dtype), *stacks)


def picked_body(channels, offsets, side, mine, other, picked, table):
    half, rows = mine.shape[0], mine.shape[2]
    owners = 2 * half
    me = lax.axis_index("space")
    for block in range(owners):
        source = mine if block < half else other
        table[block] = normalized(source[block % half][:channels])

    def place(owner):
        away = jnp.bitwise_xor(me, owner)
        return jnp.bitwise_and(away, 1) * half + jnp.right_shift(away, 1)

    for block in range(half):
        q = jnp.bitwise_xor(me, 2 * block + side)
        low = table[place(jnp.maximum(q - 1, 0))][:, LANES:]
        high = table[place(jnp.minimum(q + 1, owners - 1))][:, :LANES]
        lookup = stacked_lookup(low, table[side * half + block], high)
        columns = decoded_columns((other if side else mine)[block][channels:])

        def store(k, rows_of_k, block=block):
            span = slice(block * rows, (block + 1) * rows)
            picked[k * channels : (k + 1) * channels, span] = rows_of_k

        pick_all(lookup, columns[:offsets, :], store)


def picked_kernel(channels, offsets, side, first, mine, other, *refs):
    picked, table = refs[-2:]
    segment = lax.axis_index("segment")

    @pl.when(segment == 0 if first else segment != 0)
    def _():
        picked_body(channels, offsets, side, mine, other, picked, table)


def weight_kernel(factor, picked, slopes, *refs):
    out = refs[-1]
    slopes = jnp.concatenate([slopes[i] for i in range(slopes.shape[0])], axis=1)
    offsets, channels = out.shape[0], out.shape[1]
    for k in range(offsets):
        total = lax.dot_general(
            picked[k * channels : (k + 1) * channels, :],
            slopes,
            (((1,), (1,)), ((), ())),
            preferred_element_type=F32,
        )
        for ref in refs[:-1]:
            total = total + ref[k]
        out[k] = factor * total


def last_kernel(factor, picked, slopes, before, part, x, one, two, weight_grad, grad_in):
    finish_kernel(part, x, one, two, grad_in)
    weight_kernel(factor, picked, slopes, before, weight_grad)


def lone_picked_kernel(low, own, high, row_map, picked):
    channels = own.shape[0]
    lookup = stacked_lookup(normalized(low[...]), normalized(own[...]), normalized(high[...]))
    for k in range(row_map.shape[0]):
        picked[k * channels : (k + 1) * channels, :] = pick_rows(lookup, row_map[k : k + 1, :])


def per_device(features, weights, row_map, block_count, cotangent):
    channels, rows = features.shape
    segments, count = lax.axis_size("segment"), lax.axis_size("space")
    offsets = row_map.shape[0]
    weight = weights[0]
    wide, face = (channels, rows), (channels, LANES)
    flops = 2 * offsets * channels * channels * rows
    live = (jnp.arange(rows, dtype=jnp.int32) < block_count[0] * LANES).astype(F32)[None, :]
    everyone = count == 8 and segments == 4

    current, one, two = call(
        prepare_kernel,
        "prepare",
        [struct(wide, BF16), struct(face, BF16), struct(face, BF16)],
        features,
        live,
        far=1,
        scratch=[pltpu.VMEM(wide, BF16), pltpu.SemaphoreType.DMA],
    )
    first, second = halo_pairs(segments, count)
    low, high = lax.ppermute(one, AXES, first), lax.ppermute(two, AXES, second)
    padded = -(-offsets // 16) * 16
    weight, row_map, coded = call(
        load_kernel,
        "load",
        [
            struct(weight.shape, BF16),
            struct(row_map.shape, jnp.int32),
            struct((padded, rows), BF16),
        ],
        weight,
        row_map,
        current,
        far=2,
        scratch=[pltpu.SemaphoreType.DMA((2,))],
    )
    cores = [(p, p ^ 1) for p in range(count)]
    block, half_block = (channels + padded, rows), (channels + padded, LANES)
    message = [struct(block, BF16), struct(half_block, BF16), struct(half_block, BF16)]
    received = []

    def assemble(name, numbers, *others):
        used = 1 + max(came for number in numbers for came, _ in CAME[number])
        arrays = sum(received[:used], ())
        return call(
            functools.partial(assemble_kernel, numbers),
            name,
            struct((count // 2,) + block, BF16),
            x,
            coded,
            *after_all(arrays, others),
        )

    def pick(side, first, mine, other, *before):
        return call(
            functools.partial(picked_kernel, channels, offsets, side, first),
            f"picked{side}{'early' if first else 'late'}",
            struct((offsets * channels, count // 2 * rows), BF16),
            mine,
            other,
            *before,
            limit=24 << 20,
            scratch=[pltpu.VMEM((count, channels, rows), BF16)],
            flops=4 * flops,
            aliases={2: 0} if before else {},
        )

    z = jnp.zeros(wide, F32)
    x = act = own = current
    picked = []
    for turn in range(segments):
        outputs = call(
            functools.partial(forward_kernel, turn),
            f"forward{turn}",
            message
            + [struct(wide, F32), struct(wide, BF16), struct(wide, BF16)]
            + [struct(wide, BF16)] * (turn + 1 == segments),
            own,
            low,
            high,
            weight,
            row_map,
            coded,
            live,
            z,
            x,
            act,
            scratch=[pltpu.VMEM((offsets * channels, rows), BF16)],
            flops=flops,
        )
        sent, (z, x, act) = outputs[:3], outputs[3:6]
        acts = outputs[-1]
        if turn == 0:
            grad = call(gradient_kernel, "gradient", struct(wide, F32), cotangent, live, x)
            hot = call(hot_kernel, "hot", struct((offsets * rows, rows), BF16), row_map, x)
        if turn + 1 < segments:
            if everyone and turn == segments - 2:
                early = assemble("early_rows", (0,), z)
                early_other = lax.ppermute(early, "space", cores)
            own, from_down, from_up = hop(
                len(received), turn, turn + 1, count, sent[1], sent[2], sent[0]
            )
            received.append((own, from_down, from_up))
            low, high = from_up, from_down

    dz = jnp.zeros(wide, BF16)
    part = grad
    out_low = out_high = jnp.zeros(face, BF16)
    for turn in reversed(range(segments)):
        own, from_high, from_low = received[-1]
        dz, grad = call(
            functools.partial(slope_kernel, turn, segments),
            f"slope{turn}",
            [struct(wide, BF16), struct(wide, F32)],
            own,
            from_low,
            from_high,
            act,
            z,
            grad,
            dz,
        )
        if turn == 0 and everyone:
            late = assemble("late_rows", tuple(range(1, segments)))
            slopes = [dz] + [
                lax.ppermute(dz, "space", [(p, p ^ (2 * m)) for p in range(count)])
                for m in range(1, count // 2)
            ]
            late_other = lax.ppermute(after(late, dz), "space", cores)
        part, out_low, out_high, *sent = call(
            functools.partial(spread_kernel, turn),
            f"spread{turn}",
            [struct(wide, F32), struct(face, BF16), struct(face, BF16)]
            + (message if turn > 0 else []),
            dz,
            grad,
            x,
            act,
            weight,
            row_map,
            hot,
            coded,
            part,
            out_low,
            out_high,
            scratch=[pltpu.VMEM((2 * channels, offsets * rows), BF16)],
            limit=16 << 20,
            flops=2 * flops,
        )
        if turn > 0:
            if everyone and len(picked) < 2:
                if not picked:
                    early_other = after(early_other, dz)
                picked.append(pick(len(picked), True, early, after(early_other, dz)))
                sent = after_all(sent, picked[-1:])
            received.append(
                hop(len(received), turn, turn - 1, count, sent[1], sent[2], sent[0])
            )

    one, two = call(
        order_kernel, "order", [struct(face, BF16), struct(face, BF16)], out_low, out_high
    )
    face_one, face_two = lax.ppermute(one, AXES, first), lax.ppermute(two, AXES, second)

    factor = 1.0 / math.sqrt(rows * count)
    shape = struct((offsets, channels, channels), F32)
    if everyone:
        picked = [pick(side, False, late, late_other, picked[side]) for side in range(2)]
        slopes = after_all(slopes, (one, two, picked[0]))
        slopes = join("slopes", *(block[None] for block in slopes))
        others = lax.ppermute(slopes, "space", cores)
        weight_grad = call(
            functools.partial(weight_kernel, 1.0),
            "weight_grad_mine",
            shape,
            picked[0],
            slopes,
            limit=24 << 20,
            flops=4 * flops,
        )
        face_one, face_two = after_all((face_one, face_two), (weight_grad, picked[1]))
        weight_grad, grad_in = call(
            functools.partial(last_kernel, factor),
            "last",
            [shape, struct(wide, BF16)],
            picked[1],
            others,
            weight_grad,
            part,
            x,
            face_one,
            face_two,
            limit=24 << 20,
            flops=4 * flops,
        )
    else:
        low = lax.ppermute(x[:, LANES:], "space", [(p, p + 1) for p in range(count - 1)])
        high = lax.ppermute(x[:, :LANES], "space", [(p, p - 1) for p in range(1, count)])
        picked = call(
            lone_picked_kernel,
            "lone_picked",
            struct((offsets * channels, rows), BF16),
            low,
            x,
            high,
            row_map,
        )
        weight_grad = call(
            functools.partial(weight_kernel, factor), "weight_grad", shape, picked, dz[None]
        )
        weight_grad = lax.psum(weight_grad, "space")
        grad_in = call(finish_kernel, "finish", struct(wide, BF16), part, x, face_one, face_two)
    return acts[None], grad_in[None], weight_grad[None]


def solution(mesh):
    placed = (
        P(None, "space"),
        P("segment", None, None, None),
        P(None, "space"),
        P("space"),
        P(None, "space"),
    )
    return jax.shard_map(
        per_device,
        mesh=mesh,
        in_specs=placed,
        out_specs=(
            P("segment", None, "space"),
            P("segment", None, "space"),
            P("segment", None, None, None),
        ),
        check_vma=False,
    )
```
